128 devices in a mesh: sub: 32 (over x, y, core), rep: 4 (over z).
Axes of the slice: x: 4, y: 4, z: 4, core: 2. Of those that a mesh axis runs over, the one named last changes fastest.
Arguments:
- loads: bfloat16 [256, 256, 1024], P('sub', 'rep'), may hold values from -6 to 6
- operators: bfloat16 [256, 1024, 1024], P('sub'), may hold values from -0.1875 to 0.1875
- owner: int32 [2048, 1], P('sub'), may hold values from 0 to 31; in each aligned block of 64 rows (0 to 63, 64 to 127, ...) at most 4 rows name the same one
- dual_block: int32 [2048], P('sub'), may hold values from 0 to 15
- scale_index: int32 [65536], P('sub'), may hold values from 0 to 3
- basis: bfloat16 [65536, 1024], P('sub'), may hold values from -0.0234375 to 0.0234375
- coarse: bfloat16 [1024, 1024], replicated, may hold values from -1.5 to 1.5
Outputs:
- start: float32 [256, 65536], P('rep', 'sub')
- resid: float32 [256, 65536], P('rep', 'sub')
The draws below stay inside these ranges and needn't reach their ends.
Inputs may be any that keep to these rules, and one draw needn't show every extreme that they name: Among the blocks of the subdomains of one index of sub (aligned blocks of 64 rows), no owner is named more than 4 times, a bound that some block reaches.
All inputs are finite; a program needn't handle non-finite values.
Results may differ from the reference program's by a relative error of at most 0.0075.
Values may be sent and summed in bfloat16 or wider, within the bound.
No kernel may reach another device: no remote copies, remote signals or barrier semaphores. Data moves between devices by JAX's collectives and lax.ppermute only.
A program may use at most 128 MiB of HBM per device.

```python
import math
import jax
import jax.numpy as jnp
import numpy as np
from jax import lax

L = 1024
BLK = 128
NB = 1024
K = 256
SUB_DEV = 8
OB = 16
BPS = 8
CAP = 4
SUBS = 256
NDUAL = 65536
N_SUB = 32


def plant(values, rng, smallest, top_value):
    place = [jax.random.randint(jax.random.fold_in(rng, axis), (), 0, length) for axis, length in enumerate(values.shape)]
    widest = values.shape.index(max(values.shape))
    beside = place[:widest] + [(place[widest] + 1) % values.shape[widest]] + place[widest + 1:]
    return values.at[tuple(place)].set(smallest).at[tuple(beside)].set(top_value)


def level_of(own_key, extent, shards, smallest, largest):
    factor_of = 1.0
    for axis_at, parts in shards:
        heights = jax.random.uniform(jax.random.fold_in(jax.random.fold_in(own_key, 6), axis_at), (parts,), jnp.float32, smallest / len(shards), largest / len(shards))
        factor_of = factor_of * jnp.repeat(jnp.exp(heights), extent[axis_at] // parts).reshape((-1,) + (1,) * (len(extent) - 1 - axis_at))
    return factor_of


def deal_out(key, own, number, rows, count, top, limit, skew):
    sequence = jax.random.permutation(key, count)
    packed, ordinary = load_shares(count, rows * top, limit, skew, True), load_shares(count, rows * top, limit, skew, False)
    places = jnp.arange(count)

    def named(lengths, rotation):
        used = int((lengths > 0).sum())
        fixed = max(1, used // 4)
        moved = fixed + (places - fixed + rotation * (used - fixed)) % max(1, count - fixed)
        return jnp.zeros((count,), jnp.int32).at[sequence[jnp.where(places < fixed, places, moved)]].set(jnp.asarray(lengths, jnp.int32))

    lengths = jnp.where(number % 4 == 0, named(packed, number // 4), named(ordinary, number - number // 4 - 1))
    mixed = jax.random.permutation(jax.random.fold_in(own, 3), count)
    donor, receiver = mixed[0:count // 2 * 2:2], mixed[1:count // 2 * 2:2]
    margin = jnp.minimum(lengths[donor] - 1, limit - lengths[receiver]) // 2
    margin = jnp.where((donor == sequence[0]) | (receiver == sequence[0]) | (lengths[receiver] == 0), 0, jnp.maximum(margin, 0))
    moved = jax.random.randint(jax.random.fold_in(own, 4), (count // 2,), 0, 1 << 20) % (margin + 1)
    lengths = lengths.at[donor].add(-moved).at[receiver].add(moved)
    items = jnp.searchsorted(jnp.cumsum(lengths), jnp.arange(rows * top), side="right").astype(jnp.int32)
    grid = items.reshape(top, rows).T
    grid = grid[jax.random.permutation(jax.random.fold_in(own, 1), rows)]
    rotation = jax.random.randint(jax.random.fold_in(own, 2), (rows, 1), 0, top)
    return jnp.take_along_axis(grid, (jnp.arange(top)[None, :] + rotation) % top, axis=1)


def load_shares(number_of, total, bound, skew, full):
    weights = [(1 << 20) // math.isqrt(grade ** skew) + 1 for grade in range(1, number_of + 1)]
    largest = bound if full else min(bound, max(-(-total // number_of), total * weights[0] // sum(weights)))
    least = 1 if total - largest >= number_of - 1 else 0
    counts, spare = [largest] + [least] * (number_of - 1), total - largest - least * (number_of - 1)
    while spare > 0:
        candidates = [i for i in range(1, number_of) if counts[i] < largest] or [i for i in range(1, number_of) if counts[i] < bound]
        pool, budget = sum([weights[i] for i in candidates]), spare
        for i in candidates:
            addition = min(bound - counts[i], max(1, budget * weights[i] // pool), spare)
            counts[i] = counts[i] + addition
            spare = spare - addition
    return np.array(counts)


def gaussian(stream_key, extent, deviation, limit, shards=(), kind=jnp.bfloat16):
    result = deviation * jax.random.normal(stream_key, extent, jnp.float32)
    if shards:
        result = result * level_of(stream_key, extent, shards, -0.22, 0.18)
    return jnp.clip(result, -limit, limit).astype(kind)


def setup_inputs(seed: int = 0) -> dict:
    key_of = jax.random.split(jax.random.key(seed), 8)
    loads = gaussian(key_of[0], (SUBS, K, L), 1.0, 6.0, ((0, 32), (1, 4)))
    operators = gaussian(key_of[1], (SUBS, L, L), L ** -0.5, 0.1875, ((0, 32),))
    owner_keys = jax.random.split(jax.random.fold_in(key_of[2], 1), (SUBS * BPS) // (SUB_DEV * BPS))
    owner_turns = jax.random.permutation(jax.random.fold_in(key_of[2], 3), (SUBS * BPS) // (SUB_DEV * BPS))
    owner = jax.vmap(lambda own, number: deal_out(jax.random.fold_in(key_of[2], 2), own, number, SUB_DEV * BPS, N_SUB, 1, CAP, 2))(owner_keys, owner_turns).reshape((SUBS * BPS, 1))
    dual_block = plant(jax.random.randint(key_of[3], (SUBS * BPS,), 0, OB), jax.random.fold_in(key_of[3], 1), 0, OB - 1).astype(jnp.int32)
    scale_index = plant(jax.random.randint(key_of[4], (NDUAL,), 0, 4), jax.random.fold_in(key_of[4], 1), 0, 3).astype(jnp.int32)
    basis = gaussian(key_of[5], (NDUAL, NB), NDUAL ** -0.5, 0.0234375, ((0, 32),))
    coarse = gaussian(key_of[6], (NB, NB), (max(1, NB * NB // NDUAL)) ** -0.5, 1.5)
    return {"loads": loads, "operators": operators, "owner": owner, "dual_block": dual_block, "scale_index": scale_index, "basis": basis, "coarse": coarse}


def apply_all(inputs, operators):
    def one(pair):
        return jnp.dot(pair[0], pair[1], preferred_element_type=jnp.float32).astype(jnp.bfloat16)
    return lax.map(one, (inputs, operators))


def to_blocks(values):
    return values.reshape(SUBS, K, BPS, BLK).transpose(0, 2, 1, 3).reshape(SUBS * BPS, K, BLK)


def collect(values, targets, weight):
    blocks = to_blocks(values).astype(jnp.float32)
    total = jnp.zeros((NDUAL // BLK, K, BLK), jnp.float32).at[targets].add(blocks)
    return total.transpose(1, 0, 2).reshape(K, NDUAL) * weight[None, :]


def reference(loads, operators, owner, dual_block, scale_index, basis, coarse):
    targets = (owner[:, 0] * OB + dual_block).astype(jnp.int32)
    weight = 1.0 / (1.0 + scale_index.astype(jnp.float32))
    terms = apply_all(loads, operators)
    dual = collect(terms, targets, weight)
    coeff = jnp.dot(dual.astype(jnp.bfloat16), basis, preferred_element_type=jnp.float32)
    solved = jnp.dot(coeff.astype(jnp.bfloat16), coarse, preferred_element_type=jnp.float32).astype(jnp.bfloat16)
    start = lax.dot_general(solved, basis, (((1,), (1,)), ((), ())), preferred_element_type=jnp.float32)
    start_blocks = start.astype(jnp.bfloat16).reshape(K, NDUAL // BLK, BLK).transpose(1, 0, 2)
    picked = start_blocks[targets]
    local = picked.reshape(SUBS, BPS, K, BLK).transpose(0, 2, 1, 3).reshape(SUBS, K, L)
    again = apply_all(local, operators)
    applied = collect(again, targets, weight)
    return start, dual - applied
```

```python
import jax
import jax.numpy as jnp
from jax import lax
from jax.experimental import pallas as pl
from jax.experimental.pallas import tpu as pltpu
from jax.sharding import PartitionSpec as P

BLK = 128
PEERS = 32
CAP = 4
COLS = 64
L = 1024
BPS = 8
NSUB = 8
NBLK = NSUB * BPS
OB = 16
NB = 1024
IDROWS = 8
SLOTROWS = CAP * COLS
BF = jnp.bfloat16
F32 = jnp.float32
ANY = pl.BlockSpec(memory_space=pl.ANY)
SMEM = pl.BlockSpec(memory_space=pltpu.SMEM)
LIMIT = 56 * 1024 * 1024


def params(**kw):
    return pltpu.CompilerParams(vmem_limit_bytes=LIMIT, **kw)


def block_copy(obuf, out, pos, sem, i):
    p = pos[i]
    return pltpu.make_async_copy(
        obuf.at[i],
        out.at[p // CAP, pl.ds(pl.multiple_of((p % CAP) * COLS, COLS), COLS)],
        sem.at[i],
    )


def send_rows(prod, s, obuf, out, pos, sem):
    for j in range(BPS):
        obuf[s * BPS + j] = prod[:, j * BLK : (j + 1) * BLK].astype(BF)
    for j in range(BPS):
        block_copy(obuf, out, pos, sem, s * BPS + j).start()


def wait_rows(obuf, out, pos, sem):
    def body(i, c):
        block_copy(obuf, out, pos, sem, i).wait()
        return c

    lax.fori_loop(0, NBLK, body, 0)


def first_kernel(owner, dual_block, loads, ops, out, pos, count, obuf, idbuf, sem, idsem):
    s = pl.program_id(0)

    @pl.when(s == 0)
    def _():
        def zero(i, c):
            count[i] = 0
            return c

        lax.fori_loop(0, PEERS, zero, 0)
        row = lax.broadcasted_iota(jnp.int32, (PEERS, BLK), 0)
        lane = lax.broadcasted_iota(jnp.int32, (PEERS, BLK), 1)
        flat = row * CAP + lane
        flat = jnp.where(lane < CAP, flat, -1)

        def rank(i, ids):
            d = owner[i]
            r = count[d]
            count[d] = r + 1
            p = d * CAP + r
            pos[i] = p
            return jnp.where(flat == p, dual_block[i], ids)

        ids = lax.fori_loop(0, NBLK, rank, jnp.full((PEERS, BLK), -1, jnp.int32))
        idbuf[...] = jnp.broadcast_to(ids.astype(F32)[:, None, :], (PEERS, IDROWS, BLK)).astype(BF)
        pltpu.make_async_copy(idbuf, out.at[:, pl.ds(SLOTROWS, IDROWS)], idsem).start()

    prod = jnp.dot(loads[0], ops[0], preferred_element_type=F32)
    send_rows(prod, s, obuf, out, pos, sem)

    @pl.when(s == NSUB - 1)
    def _():
        pltpu.make_async_copy(idbuf, out.at[:, pl.ds(SLOTROWS, IDROWS)], idsem).wait()
        wait_rows(obuf, out, pos, sem)


def first_apply(owner, dual_block, loads, operators):
    return pl.pallas_call(
        first_kernel,
        out_shape=(
            jax.ShapeDtypeStruct((PEERS, SLOTROWS + IDROWS, BLK), BF),
            jax.ShapeDtypeStruct((NBLK,), jnp.int32),
        ),
        grid_spec=pltpu.PrefetchScalarGridSpec(
            num_scalar_prefetch=2,
            grid=(NSUB,),
            in_specs=[
                pl.BlockSpec((1, COLS, L), lambda s, o, d: (s, 0, 0)),
                pl.BlockSpec((1, L, L), lambda s, o, d: (s, 0, 0)),
            ],
            out_specs=[ANY, SMEM],
            scratch_shapes=[
                pltpu.SMEM((PEERS,), jnp.int32),
                pltpu.VMEM((NBLK, COLS, BLK), BF),
                pltpu.VMEM((PEERS, IDROWS, BLK), BF),
                pltpu.SemaphoreType.DMA((NBLK,)),
                pltpu.SemaphoreType.DMA,
            ],
        ),
        compiler_params=params(),
        name="first_apply",
    )(owner, dual_block, loads, operators)


def second_kernel(pos, back, ops, out, local, obuf, sem):
    s = pl.program_id(0)
    for j in range(BPS):
        p = pos[s * BPS + j]
        local[:, j * BLK : (j + 1) * BLK] = back[
            p // CAP, pl.ds(pl.multiple_of((p % CAP) * COLS, COLS), COLS), :
        ]
    prod = jnp.dot(local[...], ops[0], preferred_element_type=F32)
    send_rows(prod, s, obuf, out, pos, sem)

    @pl.when(s == NSUB - 1)
    def _():
        wait_rows(obuf, out, pos, sem)


def second_apply(pos, back, operators):
    return pl.pallas_call(
        second_kernel,
        out_shape=jax.ShapeDtypeStruct((PEERS, SLOTROWS, BLK), BF),
        grid_spec=pltpu.PrefetchScalarGridSpec(
            num_scalar_prefetch=1,
            grid=(NSUB,),
            in_specs=[
                pl.BlockSpec((PEERS, SLOTROWS, BLK), lambda s, p: (0, 0, 0)),
                pl.BlockSpec((1, L, L), lambda s, p: (s, 0, 0)),
            ],
            out_specs=ANY,
            scratch_shapes=[
                pltpu.VMEM((COLS, L), BF),
                pltpu.VMEM((NBLK, COLS, BLK), BF),
                pltpu.SemaphoreType.DMA((NBLK,)),
            ],
        ),
        compiler_params=params(),
        name="second_apply",
    )(pos, back, operators)


def add_slots(received, ids, total):
    total[...] = jnp.zeros_like(total)

    def peer(p, c):
        for q in range(CAP):
            g = ids[p, q]

            @pl.when(g >= 0)
            def _():
                total[g] = total[g] + received[p, q * COLS : (q + 1) * COLS, :].astype(F32)

        return c

    lax.fori_loop(0, PEERS, peer, 0)


def project_kernel(received, scale, basis, coarse, dual, partial, ids_out, total, narrow, basis_v, coarse_v, idv, ids, sem):
    basis_copy = pltpu.make_async_copy(basis, basis_v, sem.at[0])
    coarse_copy = pltpu.make_async_copy(coarse, coarse_v, sem.at[1])
    basis_copy.start()
    coarse_copy.start()
    idv[...] = received[:, SLOTROWS : SLOTROWS + IDROWS, :].astype(F32)[:, 0, :].astype(jnp.int32)
    ids_copy = pltpu.make_async_copy(idv, ids, sem.at[2])
    ids_copy.start()
    ids_out[...] = idv[...]
    ids_copy.wait()
    add_slots(received, ids, total)
    weight = 1.0 / (1.0 + scale[...].astype(F32))
    for b in range(OB):
        owned = total[b] * weight[b : b + 1, :]
        dual[b] = owned
        narrow[:, b * BLK : (b + 1) * BLK] = owned.astype(BF)
    basis_copy.wait()
    coeff = jnp.dot(narrow[...], basis_v[...], preferred_element_type=F32)
    high = coeff.astype(BF)
    low = (coeff - high.astype(F32)).astype(BF)
    coarse_copy.wait()
    both = jnp.dot(jnp.concatenate([high, low], axis=0), coarse_v[...], preferred_element_type=F32)
    solved = both[:COLS] + both[COLS:]
    for a in range(8):
        for b in range(4):
            partial[a * 4 + b] = solved[a * 8 : (a + 1) * 8, b * 256 : (b + 1) * 256]


def project(received, scale, basis, coarse):
    return pl.pallas_call(
        project_kernel,
        out_shape=(
            jax.ShapeDtypeStruct((OB, COLS, BLK), F32),
            jax.ShapeDtypeStruct((PEERS, 8, 256), F32),
            jax.ShapeDtypeStruct((PEERS, BLK), jnp.int32),
        ),
        in_specs=[
            pl.BlockSpec(memory_space=pltpu.VMEM),
            pl.BlockSpec(memory_space=pltpu.VMEM),
            ANY,
            ANY,
        ],
        out_specs=[pl.BlockSpec(memory_space=pltpu.VMEM)] * 3,
        scratch_shapes=[
            pltpu.VMEM((OB, COLS, BLK), F32),
            pltpu.VMEM((COLS, OB * BLK), BF),
            pltpu.VMEM((OB * BLK, NB), BF),
            pltpu.VMEM((NB, NB), BF),
            pltpu.VMEM((PEERS, BLK), jnp.int32),
            pltpu.SMEM((PEERS, BLK), jnp.int32),
            pltpu.SemaphoreType.DMA((3,)),
        ],
        compiler_params=params(),
        name="project",
    )(received, scale, basis, coarse)


def reduce_kernel(parts, out):
    total = parts[0]
    for p in range(1, PEERS):
        total = total + parts[p]
    out[...] = jnp.broadcast_to(total.astype(BF)[None], out.shape)


def reduce_parts(parts):
    return pl.pallas_call(
        reduce_kernel,
        out_shape=jax.ShapeDtypeStruct((PEERS, 8, 256), BF),
        compiler_params=params(),
        name="reduce_parts",
    )(parts)


STEPS = 4
ROWS = OB * BLK // STEPS


def start_kernel(ids, gathered, basis, start, out, solved, blocks, sem):
    n = pl.program_id(0)

    @pl.when(n == 0)
    def _():
        for a in range(8):
            for b in range(4):
                solved[a * 8 : (a + 1) * 8, b * 256 : (b + 1) * 256] = gathered[a * 4 + b]

    value = lax.dot_general(
        solved[...], basis[...], (((1,), (1,)), ((), ())), preferred_element_type=F32
    )
    start[...] = value
    for k in range(ROWS // BLK):
        blocks[n * (ROWS // BLK) + k] = value[:, k * BLK : (k + 1) * BLK].astype(BF)

    def copy(p, q, g):
        return pltpu.make_async_copy(
            blocks.at[g], out.at[p, pl.ds(q * COLS, COLS)], sem.at[p * CAP + q]
        )

    @pl.when(n == STEPS - 1)
    def _():
        def begin(p, c):
            for q in range(CAP):
                g = ids[p, q]

                @pl.when(g >= 0)
                def _():
                    copy(p, q, g).start()

            return c

        def finish(p, c):
            for q in range(CAP):
                g = ids[p, q]

                @pl.when(g >= 0)
                def _():
                    copy(p, q, g).wait()

            return c

        lax.fori_loop(0, PEERS, begin, 0)
        lax.fori_loop(0, PEERS, finish, 0)


def start_values(ids, gathered, basis):
    return pl.pallas_call(
        start_kernel,
        out_shape=(
            jax.ShapeDtypeStruct((COLS, OB * BLK), F32),
            jax.ShapeDtypeStruct((PEERS, SLOTROWS, BLK), BF),
        ),
        grid_spec=pltpu.PrefetchScalarGridSpec(
            num_scalar_prefetch=1,
            grid=(STEPS,),
            in_specs=[
                pl.BlockSpec((PEERS, 8, 256), lambda n, i: (0, 0, 0)),
                pl.BlockSpec((ROWS, NB), lambda n, i: (n, 0)),
            ],
            out_specs=[pl.BlockSpec((COLS, ROWS), lambda n, i: (0, n)), ANY],
            scratch_shapes=[
                pltpu.VMEM((COLS, NB), BF),
                pltpu.VMEM((OB, COLS, BLK), BF),
                pltpu.SemaphoreType.DMA((PEERS * CAP,)),
            ],
        ),
        compiler_params=params(),
        name="start_values",
    )(ids, gathered, basis)


def resid_kernel(ids, received, scale, dual, resid, total):
    add_slots(received, ids, total)
    weight = 1.0 / (1.0 + scale[...].astype(F32))
    for b in range(OB):
        resid[:, b * BLK : (b + 1) * BLK] = dual[b] - total[b] * weight[b : b + 1, :]


def residual(ids, received, scale, dual):
    return pl.pallas_call(
        resid_kernel,
        out_shape=jax.ShapeDtypeStruct((COLS, OB * BLK), F32),
        in_specs=[SMEM] + [pl.BlockSpec(memory_space=pltpu.VMEM)] * 3,
        out_specs=pl.BlockSpec(memory_space=pltpu.VMEM),
        scratch_shapes=[pltpu.VMEM((OB, COLS, BLK), F32)],
        compiler_params=params(),
        name="residual",
    )(ids, received, scale, dual)


def exchange(values):
    return lax.all_to_all(values, "sub", split_axis=0, concat_axis=0, tiled=True)


def per_device(loads, operators, owner, dual_block, scale_index, basis, coarse):
    scale = scale_index.reshape(OB, BLK)
    packed, pos = first_apply(owner.reshape(NBLK), dual_block, loads, operators)
    received = exchange(packed)
    dual, partial, ids = project(received, scale, basis, coarse)
    gathered = exchange(reduce_parts(exchange(partial)))
    start, requested = start_values(ids, gathered, basis)
    again = second_apply(pos, exchange(requested), operators)
    return (start, residual(ids, exchange(again), scale, dual))


def solution(mesh):
    return jax.shard_map(
        per_device,
        mesh=mesh,
        in_specs=(
            P("sub", "rep", None),
            P("sub", None, None),
            P("sub", None),
            P("sub"),
            P("sub"),
            P("sub", None),
            P(),
        ),
        out_specs=(P("rep", "sub"), P("rep", "sub")),
        check_vma=False,
    )
```

```python
import jax
import jax.numpy as jnp
from jax import lax
from jax.experimental import pallas as pl
from jax.experimental.pallas import tpu as pltpu
from jax.sharding import PartitionSpec as P

BLK = 128
PEERS = 32
CAP = 4
COLS = 64
L = 1024
BPS = 8
NSUB = 8
NBLK = NSUB * BPS
OB = 16
NB = 1024
IDROWS = 8
SLOTROWS = CAP * COLS
BF = jnp.bfloat16
F32 = jnp.float32
HBM = pl.BlockSpec(memory_space=pl.ANY)
SMEM = pl.BlockSpec(memory_space=pltpu.SMEM)
VMEM = pl.BlockSpec(memory_space=pltpu.VMEM)
AHEAD = 4


def params(mib):
    return pltpu.CompilerParams(vmem_limit_bytes=mib * 1024 * 1024)


def in_hbm(x):
    return pltpu.with_memory_space_constraint(x, pltpu.HBM)


def in_vmem(x):
    return pltpu.with_memory_space_constraint(x, pltpu.VMEM)


def slot(ref, p):
    return ref.at[p // CAP, pl.ds(pl.multiple_of((p % CAP) * COLS, COLS), COLS)]


def first_kernel(owner, dual_block, loads, ops, out, pos, ops_v, count, loads_v, sem, load_sem):
    load_copy = pltpu.make_async_copy(loads, loads_v, load_sem)
    copies = [pltpu.make_async_copy(ops.at[s], ops_v.at[s], sem.at[s]) for s in range(NSUB)]
    load_copy.start()
    for s in range(AHEAD):
        copies[s].start()

    def zero(i, c):
        count[i] = 0
        return c

    lax.fori_loop(0, PEERS, zero, 0)
    row = lax.broadcasted_iota(jnp.int32, (PEERS, BLK), 0)
    lane = lax.broadcasted_iota(jnp.int32, (PEERS, BLK), 1)
    flat = jnp.where(lane < CAP, row * CAP + lane, -1)

    def rank(i, ids):
        d = owner[i]
        r = count[d]
        count[d] = r + 1
        p = d * CAP + r
        pos[i] = p
        return jnp.where(flat == p, dual_block[i], ids)

    ids = lax.fori_loop(0, NBLK, rank, jnp.full((PEERS, BLK), -1, jnp.int32))
    out[:, SLOTROWS : SLOTROWS + IDROWS, :] = jnp.broadcast_to(
        ids.astype(F32)[:, None, :], (PEERS, IDROWS, BLK)
    ).astype(BF)
    load_copy.wait()
    for s in range(NSUB):
        copies[s].wait()
        if s + AHEAD < NSUB:
            copies[s + AHEAD].start()
        prod = jnp.dot(loads_v[s], ops_v[s], preferred_element_type=F32)
        for j in range(BPS):
            slot(out, pos[s * BPS + j])[...] = prod[:, j * BLK : (j + 1) * BLK].astype(BF)


def first_apply(owner, dual_block, loads, operators):
    return pl.pallas_call(
        first_kernel,
        out_shape=(
            pltpu.VMEM((PEERS, SLOTROWS + IDROWS, BLK), BF),
            jax.ShapeDtypeStruct((NBLK,), jnp.int32),
            pltpu.VMEM((NSUB, L, L), BF),
        ),
        in_specs=[SMEM, SMEM, HBM, HBM],
        out_specs=[VMEM, SMEM, VMEM],
        scratch_shapes=[
            pltpu.SMEM((PEERS,), jnp.int32),
            pltpu.VMEM((NSUB, COLS, L), BF),
            pltpu.SemaphoreType.DMA((NSUB,)),
            pltpu.SemaphoreType.DMA,
        ],
        compiler_params=params(8),
        name="first_apply",
    )(owner, dual_block, in_hbm(loads), in_hbm(operators))


def second_kernel(pos, back, ops, out, local):
    for s in range(NSUB):
        for j in range(BPS):
            local[s, :, j * BLK : (j + 1) * BLK] = slot(back, pos[s * BPS + j])[...]
    for s in range(NSUB):
        prod = jnp.dot(local[s], ops[s], preferred_element_type=F32)
        for j in range(BPS):
            slot(out, pos[s * BPS + j])[...] = prod[:, j * BLK : (j + 1) * BLK].astype(BF)


def second_apply(pos, back, operators):
    return pl.pallas_call(
        second_kernel,
        out_shape=pltpu.VMEM((PEERS, SLOTROWS, BLK), BF),
        in_specs=[SMEM, VMEM, VMEM],
        out_specs=VMEM,
        scratch_shapes=[pltpu.VMEM((NSUB, COLS, L), BF)],
        compiler_params=params(8),
        name="second_apply",
    )(pos, in_vmem(back), in_vmem(operators))


def add_slots(received, ids, totals):
    for q in range(CAP):
        totals[q][...] = jnp.zeros(totals[q].shape, F32)

    def peer(p, c):
        for q in range(CAP):
            g = ids[p, q]
            g = jnp.where(g < 0, OB, g)
            totals[q][g] = totals[q][g] + received[p, q * COLS : (q + 1) * COLS, :].astype(F32)
        return c

    lax.fori_loop(0, PEERS, peer, 0, unroll=2)


def sum_totals(totals, b):
    return (totals[0][b] + totals[1][b]) + (totals[2][b] + totals[3][b])


TOTALS = [pltpu.VMEM((OB + 1, COLS, BLK), F32)] * CAP


def project_kernel(received, scale, basis, coarse, dual, partial, ids_out, t0, t1, t2, t3, narrow, idv, ids, sem):
    totals = (t0, t1, t2, t3)
    idv[...] = received[:, SLOTROWS : SLOTROWS + IDROWS, :].astype(F32)[:, 0, :].astype(jnp.int32)
    ids_copy = pltpu.make_async_copy(idv, ids, sem)
    ids_copy.start()
    ids_out[...] = idv[...]
    ids_copy.wait()
    add_slots(received, ids, totals)
    weight = 1.0 / (1.0 + scale[...].astype(F32))
    for b in range(OB):
        owned = sum_totals(totals, b) * weight[b : b + 1, :]
        dual[b] = owned
        narrow[:, b * BLK : (b + 1) * BLK] = owned.astype(BF)
    coeff = jnp.dot(narrow[...], basis[...], preferred_element_type=F32)
    high = coeff.astype(BF)
    low = (coeff - high.astype(F32)).astype(BF)
    both = jnp.dot(jnp.concatenate([high, low], axis=0), coarse[...], preferred_element_type=F32)
    solved = both[:COLS] + both[COLS:]
    for a in range(8):
        for b in range(4):
            partial[a * 4 + b] = solved[a * 8 : (a + 1) * 8, b * 256 : (b + 1) * 256]


def project(received, scale, basis, coarse):
    return pl.pallas_call(
        project_kernel,
        out_shape=(
            pltpu.VMEM((OB, COLS, BLK), F32),
            pltpu.VMEM((PEERS, 8, 256), F32),
            jax.ShapeDtypeStruct((PEERS, BLK), jnp.int32),
        ),
        in_specs=[VMEM] * 4,
        out_specs=[VMEM] * 3,
        scratch_shapes=TOTALS
        + [
            pltpu.VMEM((COLS, OB * BLK), BF),
            pltpu.VMEM((PEERS, BLK), jnp.int32),
            pltpu.SMEM((PEERS, BLK), jnp.int32),
            pltpu.SemaphoreType.DMA,
        ],
        compiler_params=params(8),
        name="project",
    )(in_vmem(received), scale, in_vmem(basis), in_vmem(coarse))


def reduce_kernel(parts, out):
    total = parts[0]
    for p in range(1, PEERS):
        total = total + parts[p]
    out[...] = jnp.broadcast_to(total.astype(BF)[None], out.shape)


def reduce_parts(parts):
    return pl.pallas_call(
        reduce_kernel,
        out_shape=pltpu.VMEM((PEERS, 8, 256), BF),
        in_specs=[VMEM],
        out_specs=VMEM,
        compiler_params=params(4),
        name="reduce_parts",
    )(in_vmem(parts))


def start_kernel(ids, gathered, basis, start, out, solved, blocks):
    for a in range(8):
        for b in range(4):
            solved[a * 8 : (a + 1) * 8, b * 256 : (b + 1) * 256] = gathered[a * 4 + b]
    value = lax.dot_general(
        solved[...], basis[...], (((1,), (1,)), ((), ())), preferred_element_type=F32
    )
    start[...] = value
    for k in range(OB):
        blocks[k] = value[:, k * BLK : (k + 1) * BLK].astype(BF)

    def peer(p, c):
        for q in range(CAP):
            g = jnp.maximum(ids[p, q], 0)
            out[p, q * COLS : (q + 1) * COLS, :] = blocks[g]
        return c

    lax.fori_loop(0, PEERS, peer, 0, unroll=2)


def start_values(ids, gathered, basis):
    return pl.pallas_call(
        start_kernel,
        out_shape=(
            jax.ShapeDtypeStruct((COLS, OB * BLK), F32),
            pltpu.VMEM((PEERS, SLOTROWS, BLK), BF),
        ),
        in_specs=[SMEM, VMEM, VMEM],
        out_specs=[VMEM, VMEM],
        scratch_shapes=[
            pltpu.VMEM((COLS, NB), BF),
            pltpu.VMEM((OB, COLS, BLK), BF),
        ],
        compiler_params=params(8),
        name="start_values",
    )(ids, in_vmem(gathered), in_vmem(basis))


def resid_kernel(ids, received, scale, dual, resid, t0, t1, t2, t3):
    totals = (t0, t1, t2, t3)
    add_slots(received, ids, totals)
    weight = 1.0 / (1.0 + scale[...].astype(F32))
    for b in range(OB):
        resid[:, b * BLK : (b + 1) * BLK] = dual[b] - sum_totals(totals, b) * weight[b : b + 1, :]


def residual(ids, received, scale, dual):
    return pl.pallas_call(
        resid_kernel,
        out_shape=jax.ShapeDtypeStruct((COLS, OB * BLK), F32),
        in_specs=[SMEM] + [VMEM] * 3,
        out_specs=VMEM,
        scratch_shapes=TOTALS,
        compiler_params=params(8),
        name="residual",
    )(ids, in_vmem(received), scale, in_vmem(dual))


def exchange(values):
    return lax.all_to_all(values, "sub", split_axis=0, concat_axis=0, tiled=True)


def per_device(loads, operators, owner, dual_block, scale_index, basis, coarse):
    scale = scale_index.reshape(OB, BLK)
    packed, pos, ops_v = first_apply(owner.reshape(NBLK), dual_block, loads, operators)
    received = exchange(packed)
    dual, partial, ids = project(received, scale, basis, coarse)
    gathered = exchange(reduce_parts(exchange(partial)))
    start, requested = start_values(ids, gathered, basis)
    again = second_apply(pos, exchange(requested), ops_v)
    return (start, residual(ids, exchange(again), scale, dual))


def solution(mesh):
    return jax.shard_map(
        per_device,
        mesh=mesh,
        in_specs=(
            P("sub", "rep", None),
            P("sub", None, None),
            P("sub", None),
            P("sub"),
            P("sub"),
            P("sub", None),
            P(),
        ),
        out_specs=(P("rep", "sub"), P("rep", "sub")),
        check_vma=False,
    )
```

```python
import jax
import jax.numpy as jnp
from jax import lax
from jax.experimental import pallas as pl
from jax.experimental.pallas import tpu as pltpu
from jax.sharding import PartitionSpec as P

BLK = 128
PEERS = 32
CAP = 4
COLS = 64
HALF = COLS // 2
L = 1024
BPS = 8
NSUB = 8
NBLK = NSUB * BPS
OB = 16
NB = 1024
IDROWS = 8
SLOTROWS = CAP * COLS
BF = jnp.bfloat16
F32 = jnp.float32
HBM = pl.BlockSpec(memory_space=pl.ANY)
SMEM = pl.BlockSpec(memory_space=pltpu.SMEM)
VMEM = pl.BlockSpec(memory_space=pltpu.VMEM)
AHEAD = 4


def params(mib):
    return pltpu.CompilerParams(vmem_limit_bytes=mib * 1024 * 1024)


def in_hbm(x):
    return pltpu.with_memory_space_constraint(x, pltpu.HBM)


def in_vmem(x):
    return pltpu.with_memory_space_constraint(x, pltpu.VMEM)


def slot(ref, p):
    return ref.at[p // CAP, pl.ds(pl.multiple_of((p % CAP) * COLS, COLS), COLS)]


def first_kernel(owner_h, block_h, loads, ops, out, pos, ops_v, owner, dual_block, count, loads_v, sem, load_sem, idx_sem):
    owner_copy = pltpu.make_async_copy(owner_h, owner, idx_sem.at[0])
    block_copy = pltpu.make_async_copy(block_h, dual_block, idx_sem.at[1])
    owner_copy.start()
    block_copy.start()
    load_copy = pltpu.make_async_copy(loads, loads_v, load_sem)
    copies = [pltpu.make_async_copy(ops.at[s], ops_v.at[s], sem.at[s]) for s in range(NSUB)]
    load_copy.start()
    for s in range(AHEAD):
        copies[s].start()

    def zero(i, c):
        count[i] = 0
        return c

    lax.fori_loop(0, PEERS, zero, 0)
    owner_copy.wait()
    block_copy.wait()
    row = lax.broadcasted_iota(jnp.int32, (PEERS, BLK), 0)
    lane = lax.broadcasted_iota(jnp.int32, (PEERS, BLK), 1)
    flat = jnp.where(lane < CAP, row * CAP + lane, -1)

    def rank(i, ids):
        d = owner[i]
        r = count[d]
        count[d] = r + 1
        p = d * CAP + r
        pos[i] = p
        return jnp.where(flat == p, dual_block[i], ids)

    ids = lax.fori_loop(0, NBLK, rank, jnp.full((PEERS, BLK), -1, jnp.int32))
    out[:, SLOTROWS : SLOTROWS + IDROWS, :] = jnp.broadcast_to(
        ids.astype(F32)[:, None, :], (PEERS, IDROWS, BLK)
    ).astype(BF)
    load_copy.wait()
    for s in range(NSUB):
        copies[s].wait()
        if s + AHEAD < NSUB:
            copies[s + AHEAD].start()
        prod = jnp.dot(loads_v[s], ops_v[s], preferred_element_type=F32)
        for j in range(BPS):
            slot(out, pos[s * BPS + j])[...] = prod[:, j * BLK : (j + 1) * BLK].astype(BF)


def first_apply(owner, dual_block, loads, operators):
    return pl.pallas_call(
        first_kernel,
        out_shape=(
            pltpu.VMEM((PEERS, SLOTROWS + IDROWS, BLK), BF),
            jax.ShapeDtypeStruct((NBLK,), jnp.int32),
            pltpu.VMEM((NSUB, L, L), BF),
        ),
        in_specs=[HBM] * 4,
        out_specs=[VMEM, SMEM, VMEM],
        scratch_shapes=[
            pltpu.SMEM((NBLK,), jnp.int32),
            pltpu.SMEM((NBLK,), jnp.int32),
            pltpu.SMEM((PEERS,), jnp.int32),
            pltpu.VMEM((NSUB, COLS, L), BF),
            pltpu.SemaphoreType.DMA((NSUB,)),
            pltpu.SemaphoreType.DMA,
            pltpu.SemaphoreType.DMA((2,)),
        ],
        compiler_params=params(8),
        name="first_apply",
    )(in_hbm(owner), in_hbm(dual_block), in_hbm(loads), in_hbm(operators))


def second_kernel(pos, back, ops, out, local):
    for s in range(NSUB):
        for j in range(BPS):
            local[s, :, j * BLK : (j + 1) * BLK] = slot(back, pos[s * BPS + j])[...]
    for s in range(NSUB):
        prod = jnp.dot(local[s], ops[s], preferred_element_type=F32)
        for j in range(BPS):
            slot(out, pos[s * BPS + j])[...] = prod[:, j * BLK : (j + 1) * BLK].astype(BF)


def second_apply(pos, back, operators):
    return pl.pallas_call(
        second_kernel,
        out_shape=pltpu.VMEM((PEERS, SLOTROWS, BLK), BF),
        in_specs=[SMEM, VMEM, VMEM],
        out_specs=VMEM,
        scratch_shapes=[pltpu.VMEM((NSUB, COLS, L), BF)],
        compiler_params=params(8),
        name="second_apply",
    )(pos, in_vmem(back), in_vmem(operators))


def add_slots(received, ids, totals):
    for q in range(CAP):
        totals[q][...] = jnp.zeros(totals[q].shape, F32)

    def peer(p, c):
        for q in range(CAP):
            g = ids[p, q]
            g = jnp.where(g < 0, OB, g)
            totals[q][g] = totals[q][g] + received[p, q * COLS : (q + 1) * COLS, :].astype(F32)
        return c

    lax.fori_loop(0, PEERS, peer, 0, unroll=2)


def sum_totals(totals, b):
    return (totals[0][b] + totals[1][b]) + (totals[2][b] + totals[3][b])


TOTALS = [pltpu.VMEM((OB + 1, COLS, BLK), F32)] * CAP


def project_kernel(received, scale, basis, coarse, dual, keep, send, ids_out, t0, t1, t2, t3, narrow, solved, idv, ids, sem):
    totals = (t0, t1, t2, t3)
    idv[...] = received[:, SLOTROWS : SLOTROWS + IDROWS, :].astype(F32)[:, 0, :].astype(jnp.int32)
    ids_copy = pltpu.make_async_copy(idv, ids, sem)
    ids_copy.start()
    ids_out[...] = idv[...]
    ids_copy.wait()
    add_slots(received, ids, totals)
    weight = 1.0 / (1.0 + scale[...].astype(F32))
    for b in range(OB):
        owned = sum_totals(totals, b) * weight[b : b + 1, :]
        dual[b] = owned
        narrow[:, b * BLK : (b + 1) * BLK] = owned.astype(BF)
    coeff = jnp.dot(narrow[...], basis[...], preferred_element_type=F32)
    high = coeff.astype(BF)
    low = (coeff - high.astype(F32)).astype(BF)
    both = jnp.dot(jnp.concatenate([high, low], axis=0), coarse[...], preferred_element_type=F32)
    solved[0] = both[:HALF] + both[COLS : COLS + HALF]
    solved[1] = both[HALF:COLS] + both[COLS + HALF :]
    core = lax.axis_index("sub") % 2
    keep[...] = solved[core]
    send[...] = solved[1 - core]


def project(received, scale, basis, coarse):
    return pl.pallas_call(
        project_kernel,
        out_shape=(
            pltpu.VMEM((OB, COLS, BLK), F32),
            pltpu.VMEM((HALF, NB), F32),
            pltpu.VMEM((HALF, NB), F32),
            jax.ShapeDtypeStruct((PEERS, BLK), jnp.int32),
        ),
        in_specs=[VMEM] * 4,
        out_specs=[VMEM] * 4,
        scratch_shapes=TOTALS
        + [
            pltpu.VMEM((COLS, OB * BLK), BF),
            pltpu.VMEM((2, HALF, NB), F32),
            pltpu.VMEM((PEERS, BLK), jnp.int32),
            pltpu.SMEM((PEERS, BLK), jnp.int32),
            pltpu.SemaphoreType.DMA,
        ],
        compiler_params=params(8),
        name="project",
    )(in_vmem(received), scale, in_vmem(basis), in_vmem(coarse))


def add_kernel(own, *refs):
    total = own[...]
    for other in refs[:-2]:
        total = total + other[...].astype(F32)
    refs[-2][...] = total
    refs[-1][...] = total.astype(BF)


def add_parts(own, others):
    return pl.pallas_call(
        add_kernel,
        out_shape=(pltpu.VMEM((HALF, NB), F32), pltpu.VMEM((HALF, NB), BF)),
        in_specs=[VMEM] * (1 + len(others)),
        out_specs=[VMEM] * 2,
        compiler_params=params(4),
        name="add_parts",
    )(in_vmem(own), *[in_vmem(o) for o in others])


def shifted(values, dx, dy, dc):
    pairs = []
    for i in range(PEERS):
        x, y, c = i // 8, i // 2 % 4, i % 2
        pairs.append((i, (x + dx) % 4 * 8 + (y + dy) % 4 * 2 + (c + dc) % 2))
    return lax.ppermute(values, "sub", pairs)


def sum_over_owners(keep, send):
    total, narrow = add_parts(keep, [shifted(send, 0, 0, 1)])
    total, narrow = add_parts(total, [shifted(narrow, k, 0, 0) for k in (2, 1, 3)])
    total, narrow = add_parts(total, [shifted(narrow, 0, k, 0) for k in (2, 1, 3)])
    return narrow, shifted(narrow, 0, 0, 1)


def start_kernel(ids, own, other, basis, start, out, solved, blocks):
    core = lax.axis_index("sub") % 2
    solved[core] = own[...]
    solved[1 - core] = other[...]
    value = lax.dot_general(
        solved[...].reshape(COLS, NB), basis[...], (((1,), (1,)), ((), ())), preferred_element_type=F32
    )
    start[...] = value
    for k in range(OB):
        blocks[k] = value[:, k * BLK : (k + 1) * BLK].astype(BF)

    def peer(p, c):
        for q in range(CAP):
            g = jnp.maximum(ids[p, q], 0)
            out[p, q * COLS : (q + 1) * COLS, :] = blocks[g]
        return c

    lax.fori_loop(0, PEERS, peer, 0, unroll=2)


def start_values(ids, own, other, basis):
    return pl.pallas_call(
        start_kernel,
        out_shape=(
            jax.ShapeDtypeStruct((COLS, OB * BLK), F32),
            pltpu.VMEM((PEERS, SLOTROWS, BLK), BF),
        ),
        in_specs=[SMEM, VMEM, VMEM, VMEM],
        out_specs=[VMEM, VMEM],
        scratch_shapes=[
            pltpu.VMEM((2, HALF, NB), BF),
            pltpu.VMEM((OB, COLS, BLK), BF),
        ],
        compiler_params=params(8),
        name="start_values",
    )(ids, in_vmem(own), in_vmem(other), in_vmem(basis))


def resid_kernel(ids, received, scale, dual, resid, t0, t1, t2, t3):
    totals = (t0, t1, t2, t3)
    add_slots(received, ids, totals)
    weight = 1.0 / (1.0 + scale[...].astype(F32))
    for b in range(OB):
        resid[:, b * BLK : (b + 1) * BLK] = dual[b] - sum_totals(totals, b) * weight[b : b + 1, :]


def residual(ids, received, scale, dual):
    return pl.pallas_call(
        resid_kernel,
        out_shape=jax.ShapeDtypeStruct((COLS, OB * BLK), F32),
        in_specs=[SMEM] + [VMEM] * 3,
        out_specs=VMEM,
        scratch_shapes=TOTALS,
        compiler_params=params(8),
        name="residual",
    )(ids, in_vmem(received), scale, in_vmem(dual))


def exchange(values):
    return lax.all_to_all(values, "sub", split_axis=0, concat_axis=0, tiled=True)


def per_device(loads, operators, owner, dual_block, scale_index, basis, coarse):
    scale = scale_index.reshape(OB, BLK)
    packed, pos, ops_v = first_apply(owner.reshape(NBLK), dual_block, loads, operators)
    received = exchange(packed)
    dual, keep, send, ids = project(received, scale, basis, coarse)
    own, other = sum_over_owners(keep, send)
    start, requested = start_values(ids, own, other, basis)
    again = second_apply(pos, exchange(requested), ops_v)
    return (start, residual(ids, exchange(again), scale, dual))


def solution(mesh):
    return jax.shard_map(
        per_device,
        mesh=mesh,
        in_specs=(
            P("sub", "rep", None),
            P("sub", None, None),
            P("sub", None),
            P("sub"),
            P("sub"),
            P("sub", None),
            P(),
        ),
        out_specs=(P("rep", "sub"), P("rep", "sub")),
        check_vma=False,
    )
```

```python
import functools

import jax
import jax.numpy as jnp
from jax import lax
from jax.experimental import pallas as pl
from jax.experimental.pallas import tpu as pltpu
from jax.sharding import PartitionSpec as P

BLK = 128
PEERS = 32
CAP = 4
COLS = 64
HALF = COLS // 2
L = 1024
BPS = 8
NSUB = 8
NBLK = NSUB * BPS
OB = 16
MERGE = OB * BLK // 2
NB = 1024
IDROWS = 8
SLOTROWS = CAP * COLS
BF = jnp.bfloat16
F32 = jnp.float32
HBM = pl.BlockSpec(memory_space=pl.ANY)
SMEM = pl.BlockSpec(memory_space=pltpu.SMEM)
VMEM = pl.BlockSpec(memory_space=pltpu.VMEM)
AHEAD = 4


def params(mib):
    return pltpu.CompilerParams(vmem_limit_bytes=mib * 1024 * 1024)


def in_hbm(x):
    return pltpu.with_memory_space_constraint(x, pltpu.HBM)


def in_vmem(x):
    return pltpu.with_memory_space_constraint(x, pltpu.VMEM)


def slot(ref, p):
    return ref.at[p // CAP, pl.ds(pl.multiple_of((p % CAP) * COLS, COLS), COLS)]


def first_kernel(owner_h, block_h, loads, ops, out, pos, ops_v, owner, dual_block, count, loads_v, sem, load_sem, idx_sem):
    owner_copy = pltpu.make_async_copy(owner_h, owner, idx_sem.at[0])
    block_copy = pltpu.make_async_copy(block_h, dual_block, idx_sem.at[1])
    owner_copy.start()
    block_copy.start()
    load_copy = pltpu.make_async_copy(loads, loads_v, load_sem)
    copies = [pltpu.make_async_copy(ops.at[s], ops_v.at[s], sem.at[s]) for s in range(NSUB)]
    load_copy.start()
    for s in range(AHEAD):
        copies[s].start()

    def zero(i, c):
        count[i] = 0
        return c

    lax.fori_loop(0, PEERS, zero, 0)
    owner_copy.wait()
    block_copy.wait()
    row = lax.broadcasted_iota(jnp.int32, (PEERS, BLK), 0)
    lane = lax.broadcasted_iota(jnp.int32, (PEERS, BLK), 1)
    flat = jnp.where(lane < CAP, row * CAP + lane, -1)

    def rank(i, ids):
        d = owner[i]
        r = count[d]
        count[d] = r + 1
        p = d * CAP + r
        pos[i] = p
        return jnp.where(flat == p, dual_block[i], ids)

    ids = lax.fori_loop(0, NBLK, rank, jnp.full((PEERS, BLK), -1, jnp.int32))
    out[:, SLOTROWS : SLOTROWS + IDROWS, :] = jnp.broadcast_to(
        ids.astype(F32)[:, None, :], (PEERS, IDROWS, BLK)
    ).astype(BF)
    load_copy.wait()
    for s in range(NSUB):
        copies[s].wait()
        if s + AHEAD < NSUB:
            copies[s + AHEAD].start()
        prod = jnp.dot(loads_v[s], ops_v[s], preferred_element_type=F32)
        for j in range(BPS):
            slot(out, pos[s * BPS + j])[...] = prod[:, j * BLK : (j + 1) * BLK].astype(BF)


def first_apply(owner, dual_block, loads, operators):
    return pl.pallas_call(
        first_kernel,
        out_shape=(
            pltpu.VMEM((PEERS, SLOTROWS + IDROWS, BLK), BF),
            jax.ShapeDtypeStruct((NBLK,), jnp.int32),
            pltpu.VMEM((NSUB, L, L), BF),
        ),
        in_specs=[HBM] * 4,
        out_specs=[VMEM, SMEM, VMEM],
        scratch_shapes=[
            pltpu.SMEM((NBLK,), jnp.int32),
            pltpu.SMEM((NBLK,), jnp.int32),
            pltpu.SMEM((PEERS,), jnp.int32),
            pltpu.VMEM((NSUB, COLS, L), BF),
            pltpu.SemaphoreType.DMA((NSUB,)),
            pltpu.SemaphoreType.DMA,
            pltpu.SemaphoreType.DMA((2,)),
        ],
        compiler_params=params(8),
        name="first_apply",
    )(in_hbm(owner), in_hbm(dual_block), in_hbm(loads), in_hbm(operators))


def second_kernel(pos, back, ops, out, local):
    for s in range(NSUB):
        for j in range(BPS):
            local[s, :, j * BLK : (j + 1) * BLK] = slot(back, pos[s * BPS + j])[...]
    for s in range(NSUB):
        prod = jnp.dot(local[s], ops[s], preferred_element_type=F32)
        for j in range(BPS):
            slot(out, pos[s * BPS + j])[...] = prod[:, j * BLK : (j + 1) * BLK].astype(BF)


def second_apply(pos, back, operators):
    return pl.pallas_call(
        second_kernel,
        out_shape=pltpu.VMEM((PEERS, SLOTROWS, BLK), BF),
        in_specs=[SMEM, VMEM, VMEM],
        out_specs=VMEM,
        scratch_shapes=[pltpu.VMEM((NSUB, COLS, L), BF)],
        compiler_params=params(8),
        name="second_apply",
    )(pos, in_vmem(back), in_vmem(operators))


def merge_kernel(part, coarse, basis, after, merged):
    for k in range(4):
        rows = slice(part * MERGE + k * 256, part * MERGE + (k + 1) * 256)
        merged[:, k * 256 : (k + 1) * 256] = lax.dot_general(
            coarse[...], basis[rows, :], (((1,), (1,)), ((), ())), preferred_element_type=F32
        ).astype(BF)


def merge(part, coarse, basis, after):
    return pl.pallas_call(
        functools.partial(merge_kernel, part),
        out_shape=pltpu.VMEM((NB, MERGE), BF),
        in_specs=[VMEM] * 3,
        out_specs=VMEM,
        compiler_params=params(6),
        name="merge",
    )(in_vmem(coarse), in_vmem(basis), in_vmem(after))


def add_slots(received, ids, totals):
    for q in range(CAP):
        totals[q][...] = jnp.zeros(totals[q].shape, F32)

    def peer(p, c):
        for q in range(CAP):
            g = ids[p, q]
            g = jnp.where(g < 0, OB, g)
            totals[q][g] = totals[q][g] + received[p, q * COLS : (q + 1) * COLS, :].astype(F32)
        return c

    lax.fori_loop(0, PEERS, peer, 0, unroll=2)


def sum_totals(totals, b):
    return (totals[0][b] + totals[1][b]) + (totals[2][b] + totals[3][b])


TOTALS = [pltpu.VMEM((OB + 1, COLS, BLK), F32)] * CAP


def project_kernel(received, scale, basis, coarse, dual, keep, send, ids_out, coarse_v, t0, t1, t2, t3, narrow, coeff, idv, ids, sem, coarse_sem):
    coarse_copy = pltpu.make_async_copy(coarse, coarse_v, coarse_sem)
    coarse_copy.start()
    totals = (t0, t1, t2, t3)
    idv[...] = received[:, SLOTROWS : SLOTROWS + IDROWS, :].astype(F32)[:, 0, :].astype(jnp.int32)
    ids_copy = pltpu.make_async_copy(idv, ids, sem)
    ids_copy.start()
    ids_out[...] = idv[...]
    ids_copy.wait()
    add_slots(received, ids, totals)
    weight = 1.0 / (1.0 + scale[...].astype(F32))
    for b in range(OB):
        owned = sum_totals(totals, b) * weight[b : b + 1, :]
        dual[b] = owned
        narrow[:, b * BLK : (b + 1) * BLK] = owned.astype(BF)
    product = jnp.dot(narrow[...], basis[...], preferred_element_type=F32)
    coeff[0] = product[:HALF]
    coeff[1] = product[HALF:]
    core = lax.axis_index("sub") % 2
    keep[...] = coeff[core]
    send[...] = coeff[1 - core]
    coarse_copy.wait()


def project(received, scale, basis, coarse):
    return pl.pallas_call(
        project_kernel,
        out_shape=(
            pltpu.VMEM((OB, COLS, BLK), F32),
            pltpu.VMEM((HALF, NB), F32),
            pltpu.VMEM((HALF, NB), F32),
            jax.ShapeDtypeStruct((PEERS, BLK), jnp.int32),
            pltpu.VMEM((NB, NB), BF),
        ),
        in_specs=[VMEM] * 3 + [HBM],
        out_specs=[VMEM] * 5,
        scratch_shapes=TOTALS
        + [
            pltpu.VMEM((COLS, OB * BLK), BF),
            pltpu.VMEM((2, HALF, NB), F32),
            pltpu.VMEM((PEERS, BLK), jnp.int32),
            pltpu.SMEM((PEERS, BLK), jnp.int32),
            pltpu.SemaphoreType.DMA,
            pltpu.SemaphoreType.DMA,
        ],
        compiler_params=params(8),
        name="project",
    )(in_vmem(received), scale, in_vmem(basis), in_hbm(coarse))


def add_kernel(count, inputs, *refs):
    total = refs[0][...]
    for other in refs[1:count]:
        total = total + other[...].astype(F32)
    for out in refs[inputs:]:
        out[...] = total.astype(out.dtype)


def add_parts(own, others, types, after=()):
    count = 1 + len(others)
    inputs = count + len(after)
    return pl.pallas_call(
        functools.partial(add_kernel, count, inputs),
        out_shape=[pltpu.VMEM((HALF, NB), t) for t in types],
        in_specs=[VMEM] * inputs,
        out_specs=[VMEM] * len(types),
        compiler_params=params(4),
        name="add_parts",
    )(in_vmem(own), *[in_vmem(o) for o in (*others, *after)])


def shifted(values, dx, dy, dc):
    pairs = []
    for i in range(PEERS):
        x, y, c = i // 8, i // 2 % 4, i % 2
        pairs.append((i, (x + dx) % 4 * 8 + (y + dy) % 4 * 2 + (c + dc) % 2))
    return lax.ppermute(values, "sub", pairs)


def sum_over_owners(keep, send, coarse, basis):
    both = (F32, BF)
    total, narrow = add_parts(keep, [shifted(send, 0, 0, 1)], both)
    first = merge(0, coarse, basis, narrow)
    others = [shifted(narrow, k, 0, 0) for k in (3, 1, 2)]
    total, narrow = add_parts(total, others, both, (first,))
    second = merge(1, coarse, basis, narrow)
    others = [shifted(narrow, 0, k, 0) for k in (3, 1, 2)]
    (narrow,) = add_parts(total, others, (BF,), (second,))
    return narrow, shifted(narrow, 0, 0, 1), first, second


def start_kernel(ids, own, other, first, second, start, out, coeff, blocks):
    core = lax.axis_index("sub") % 2
    coeff[core] = own[...]
    coeff[1 - core] = other[...]
    for part, merged in enumerate((first, second)):
        value = jnp.dot(coeff[...].reshape(COLS, NB), merged[...], preferred_element_type=F32)
        start[:, part * MERGE : (part + 1) * MERGE] = value
        for k in range(MERGE // BLK):
            blocks[part * (MERGE // BLK) + k] = value[:, k * BLK : (k + 1) * BLK].astype(BF)

    def peer(p, c):
        for q in range(CAP):
            g = jnp.maximum(ids[p, q], 0)
            out[p, q * COLS : (q + 1) * COLS, :] = blocks[g]
        return c

    lax.fori_loop(0, PEERS, peer, 0, unroll=2)


def start_values(ids, own, other, first, second):
    return pl.pallas_call(
        start_kernel,
        out_shape=(
            jax.ShapeDtypeStruct((COLS, OB * BLK), F32),
            pltpu.VMEM((PEERS, SLOTROWS, BLK), BF),
        ),
        in_specs=[SMEM] + [VMEM] * 4,
        out_specs=[VMEM, VMEM],
        scratch_shapes=[
            pltpu.VMEM((2, HALF, NB), BF),
            pltpu.VMEM((OB, COLS, BLK), BF),
        ],
        compiler_params=params(8),
        name="start_values",
    )(ids, in_vmem(own), in_vmem(other), in_vmem(first), in_vmem(second))


def resid_kernel(ids, received, scale, dual, resid, t0, t1, t2, t3):
    totals = (t0, t1, t2, t3)
    add_slots(received, ids, totals)
    weight = 1.0 / (1.0 + scale[...].astype(F32))
    for b in range(OB):
        resid[:, b * BLK : (b + 1) * BLK] = dual[b] - sum_totals(totals, b) * weight[b : b + 1, :]


def residual(ids, received, scale, dual):
    return pl.pallas_call(
        resid_kernel,
        out_shape=jax.ShapeDtypeStruct((COLS, OB * BLK), F32),
        in_specs=[SMEM] + [VMEM] * 3,
        out_specs=VMEM,
        scratch_shapes=TOTALS,
        compiler_params=params(8),
        name="residual",
    )(ids, in_vmem(received), scale, in_vmem(dual))


def exchange(values):
    return lax.all_to_all(values, "sub", split_axis=0, concat_axis=0, tiled=True)


def per_device(loads, operators, owner, dual_block, scale_index, basis, coarse):
    scale = scale_index.reshape(OB, BLK)
    packed, pos, ops_v = first_apply(owner.reshape(NBLK), dual_block, loads, operators)
    received = exchange(packed)
    dual, keep, send, ids, coarse_v = project(received, scale, basis, coarse)
    own, other, first, second = sum_over_owners(keep, send, coarse_v, basis)
    start, requested = start_values(ids, own, other, first, second)
    again = second_apply(pos, exchange(requested), ops_v)
    return (start, residual(ids, exchange(again), scale, dual))


def solution(mesh):
    return jax.shard_map(
        per_device,
        mesh=mesh,
        in_specs=(
            P("sub", "rep", None),
            P("sub", None, None),
            P("sub", None),
            P("sub"),
            P("sub"),
            P("sub", None),
            P(),
        ),
        out_specs=(P("rep", "sub"), P("rep", "sub")),
        check_vma=False,
    )
```

```python
import functools

import jax
import jax.numpy as jnp
from jax import lax
from jax.experimental import pallas as pl
from jax.experimental.pallas import tpu as pltpu
from jax.sharding import PartitionSpec as P

BLK = 128
PEERS = 32
CAP = 4
COLS = 64
HALF = COLS // 2
L = 1024
BPS = 8
NSUB = 8
NBLK = NSUB * BPS
OB = 16
MERGE = OB * BLK // 2
NB = 1024
IDROWS = 8
SLOTROWS = CAP * COLS
BF = jnp.bfloat16
F32 = jnp.float32
HBM = pl.BlockSpec(memory_space=pl.ANY)
SMEM = pl.BlockSpec(memory_space=pltpu.SMEM)
VMEM = pl.BlockSpec(memory_space=pltpu.VMEM)


def params(mib):
    return pltpu.CompilerParams(vmem_limit_bytes=mib * 1024 * 1024)


def in_hbm(x):
    return pltpu.with_memory_space_constraint(x, pltpu.HBM)


def in_vmem(x):
    return pltpu.with_memory_space_constraint(x, pltpu.VMEM)


def slot(ref, p):
    return ref.at[p // CAP, pl.ds(pl.multiple_of((p % CAP) * COLS, COLS), COLS)]


def first_kernel(owner_h, block_h, loads, ops, out, pos, ops_v, owner, dual_block, count, loads_v, sem, load_sem, idx_sem):
    owner_copy = pltpu.make_async_copy(owner_h, owner, idx_sem.at[0])
    block_copy = pltpu.make_async_copy(block_h, dual_block, idx_sem.at[1])
    owner_copy.start()
    block_copy.start()
    load_copy = pltpu.make_async_copy(loads, loads_v, load_sem)
    copies = [pltpu.make_async_copy(ops.at[s], ops_v.at[s], sem.at[s]) for s in range(NSUB - 1)]
    copies += [
        pltpu.make_async_copy(
            ops.at[NSUB - 1, pl.ds(h * (L // 2), L // 2)],
            ops_v.at[NSUB - 1, pl.ds(h * (L // 2), L // 2)],
            sem.at[NSUB - 1 + h],
        )
        for h in range(2)
    ]
    load_copy.start()
    for c in copies:
        c.start()

    def zero(i, c):
        count[i] = 0
        return c

    lax.fori_loop(0, PEERS, zero, 0)
    owner_copy.wait()
    block_copy.wait()
    row = lax.broadcasted_iota(jnp.int32, (PEERS, BLK), 0)
    lane = lax.broadcasted_iota(jnp.int32, (PEERS, BLK), 1)
    flat = jnp.where(lane < CAP, row * CAP + lane, -1)

    def rank(i, ids):
        d = owner[i]
        r = count[d]
        count[d] = r + 1
        p = d * CAP + r
        pos[i] = p
        return jnp.where(flat == p, dual_block[i], ids)

    ids = lax.fori_loop(0, NBLK, rank, jnp.full((PEERS, BLK), -1, jnp.int32))
    out[:, SLOTROWS : SLOTROWS + IDROWS, :] = jnp.broadcast_to(
        ids.astype(F32)[:, None, :], (PEERS, IDROWS, BLK)
    ).astype(BF)
    load_copy.wait()
    for s in range(NSUB):
        copies[s].wait()
        if s < NSUB - 1:
            prod = jnp.dot(loads_v[s], ops_v[s], preferred_element_type=F32)
        else:
            half = L // 2
            prod = jnp.dot(loads_v[s, :, :half], ops_v[s, :half], preferred_element_type=F32)
            copies[s + 1].wait()
            prod = prod + jnp.dot(
                loads_v[s, :, half:], ops_v[s, half:], preferred_element_type=F32
            )
        for j in range(BPS):
            slot(out, pos[s * BPS + j])[...] = prod[:, j * BLK : (j + 1) * BLK].astype(BF)


def first_apply(owner, dual_block, loads, operators):
    return pl.pallas_call(
        first_kernel,
        out_shape=(
            pltpu.VMEM((PEERS, SLOTROWS + IDROWS, BLK), BF),
            jax.ShapeDtypeStruct((NBLK,), jnp.int32),
            pltpu.VMEM((NSUB, L, L), BF),
        ),
        in_specs=[HBM] * 4,
        out_specs=[VMEM, SMEM, VMEM],
        scratch_shapes=[
            pltpu.SMEM((NBLK,), jnp.int32),
            pltpu.SMEM((NBLK,), jnp.int32),
            pltpu.SMEM((PEERS,), jnp.int32),
            pltpu.VMEM((NSUB, COLS, L), BF),
            pltpu.SemaphoreType.DMA((NSUB + 1,)),
            pltpu.SemaphoreType.DMA,
            pltpu.SemaphoreType.DMA((2,)),
        ],
        compiler_params=params(8),
        name="first_apply",
    )(in_hbm(owner), in_hbm(dual_block), in_hbm(loads), in_hbm(operators))


def second_kernel(pos, back, ops, out, local):
    for s in range(NSUB):
        for j in range(BPS):
            local[s, :, j * BLK : (j + 1) * BLK] = slot(back, pos[s * BPS + j])[...]
    for s in range(NSUB):
        prod = jnp.dot(local[s], ops[s], preferred_element_type=F32)
        for j in range(BPS):
            slot(out, pos[s * BPS + j])[...] = prod[:, j * BLK : (j + 1) * BLK].astype(BF)


def second_apply(pos, back, operators):
    return pl.pallas_call(
        second_kernel,
        out_shape=pltpu.VMEM((PEERS, SLOTROWS, BLK), BF),
        in_specs=[SMEM, VMEM, VMEM],
        out_specs=VMEM,
        scratch_shapes=[pltpu.VMEM((NSUB, COLS, L), BF)],
        compiler_params=params(8),
        name="second_apply",
    )(pos, in_vmem(back), in_vmem(operators))


def merge_kernel(part, coarse, basis, after, merged):
    for k in range(4):
        rows = slice(part * MERGE + k * 256, part * MERGE + (k + 1) * 256)
        merged[:, k * 256 : (k + 1) * 256] = lax.dot_general(
            coarse[...], basis[rows, :], (((1,), (1,)), ((), ())), preferred_element_type=F32
        ).astype(BF)


def merge(part, coarse, basis, after):
    return pl.pallas_call(
        functools.partial(merge_kernel, part),
        out_shape=pltpu.VMEM((NB, MERGE), BF),
        in_specs=[VMEM] * 3,
        out_specs=VMEM,
        compiler_params=params(6),
        name="merge",
    )(in_vmem(coarse), in_vmem(basis), in_vmem(after))


def zero_totals(totals):
    for q in range(CAP):
        totals[q][...] = jnp.zeros(totals[q].shape, F32)


def add_slots(received, ids, totals):
    def peer(p, c):
        for q in range(CAP):
            g = ids[p, q]
            g = jnp.where(g < 0, OB, g)
            totals[q][g] = totals[q][g] + received[p, q * COLS : (q + 1) * COLS, :].astype(F32)
        return c

    lax.fori_loop(0, PEERS, peer, 0, unroll=2)


def sum_totals(totals, b):
    return (totals[0][b] + totals[1][b]) + (totals[2][b] + totals[3][b])


TOTALS = [pltpu.VMEM((OB + 1, COLS, BLK), F32)] * CAP


def project_kernel(received, scale, basis, coarse, dual, keep, send, ids_out, coarse_v, t0, t1, t2, t3, narrow, coeff, idv, ids, sem, coarse_sem):
    coarse_copy = pltpu.make_async_copy(coarse, coarse_v, coarse_sem)
    coarse_copy.start()
    totals = (t0, t1, t2, t3)
    idv[...] = received[:, SLOTROWS : SLOTROWS + IDROWS, :].astype(F32)[:, 0, :].astype(jnp.int32)
    ids_copy = pltpu.make_async_copy(idv, ids, sem)
    ids_copy.start()
    ids_out[...] = idv[...]
    zero_totals(totals)
    ids_copy.wait()
    add_slots(received, ids, totals)
    weight = 1.0 / (1.0 + scale[...].astype(F32))
    for b in range(OB):
        owned = sum_totals(totals, b) * weight[b : b + 1, :]
        dual[b] = owned
        narrow[:, b * BLK : (b + 1) * BLK] = owned.astype(BF)
    product = jnp.dot(narrow[...], basis[...], preferred_element_type=F32)
    coeff[0] = product[:HALF]
    coeff[1] = product[HALF:]
    core = lax.axis_index("sub") % 2
    keep[...] = coeff[core]
    send[...] = coeff[1 - core]
    coarse_copy.wait()


def project(received, scale, basis, coarse):
    return pl.pallas_call(
        project_kernel,
        out_shape=(
            pltpu.VMEM((OB, COLS, BLK), F32),
            pltpu.VMEM((HALF, NB), F32),
            pltpu.VMEM((HALF, NB), F32),
            pltpu.VMEM((PEERS, BLK), jnp.int32),
            pltpu.VMEM((NB, NB), BF),
        ),
        in_specs=[VMEM] * 3 + [HBM],
        out_specs=[VMEM] * 5,
        scratch_shapes=TOTALS
        + [
            pltpu.VMEM((COLS, OB * BLK), BF),
            pltpu.VMEM((2, HALF, NB), F32),
            pltpu.VMEM((PEERS, BLK), jnp.int32),
            pltpu.SMEM((PEERS, BLK), jnp.int32),
            pltpu.SemaphoreType.DMA,
            pltpu.SemaphoreType.DMA,
        ],
        compiler_params=params(8),
        name="project",
    )(in_vmem(received), scale, in_vmem(basis), in_hbm(coarse))


def add_kernel(count, inputs, *refs):
    total = refs[0][...]
    for other in refs[1:count]:
        total = total + other[...].astype(F32)
    for out in refs[inputs:]:
        out[...] = total.astype(out.dtype)


def add_parts(own, others, types, after=()):
    count = 1 + len(others)
    inputs = count + len(after)
    return pl.pallas_call(
        functools.partial(add_kernel, count, inputs),
        out_shape=[pltpu.VMEM((HALF, NB), t) for t in types],
        in_specs=[VMEM] * inputs,
        out_specs=[VMEM] * len(types),
        compiler_params=params(4),
        name="add_parts",
    )(in_vmem(own), *[in_vmem(o) for o in (*others, *after)])


def swapped(values, kx, ky, kc):
    pairs = [(i, i ^ (kx * 8 + ky * 2 + kc)) for i in range(PEERS)]
    return lax.ppermute(values, "sub", pairs)


def sum_over_owners(keep, send, coarse, basis):
    both = (F32, BF)
    total, narrow = add_parts(keep, [swapped(send, 0, 0, 1)], both)
    first = merge(0, coarse, basis, narrow)
    others = [swapped(narrow, k, 0, 0) for k in (3, 1, 2)]
    total, narrow = add_parts(total, others, both, (first,))
    second = merge(1, coarse, basis, narrow)
    others = [swapped(narrow, 0, k, 0) for k in (3, 1, 2)]
    (narrow,) = add_parts(total, others, (BF,), (second,))
    return narrow, swapped(narrow, 0, 0, 1), first, second


PIECES = 4
PIECE = OB * BLK // PIECES


def start_kernel(ids_v, own, other, first, second, start, out, coeff, blocks, value, ids, sem, ids_sem):
    ids_copy = pltpu.make_async_copy(ids_v, ids, ids_sem)
    ids_copy.start()
    core = lax.axis_index("sub") % 2
    coeff[core] = own[...]
    coeff[1 - core] = other[...]
    copies = []
    for n in range(PIECES):
        merged = (first, second)[n // 2]
        cols = slice(n % 2 * PIECE, (n % 2 + 1) * PIECE)
        value[n] = jnp.dot(
            coeff[...].reshape(COLS, NB), merged[:, cols], preferred_element_type=F32
        )
        copies.append(
            pltpu.make_async_copy(value.at[n], start.at[:, pl.ds(n * PIECE, PIECE)], sem.at[n])
        )
        copies[n].start()
        for k in range(PIECE // BLK):
            blocks[n * (PIECE // BLK) + k] = value[n, :, k * BLK : (k + 1) * BLK].astype(BF)
    ids_copy.wait()

    def peer(p, c):
        for q in range(CAP):
            g = jnp.maximum(ids[p, q], 0)
            out[p, q * COLS : (q + 1) * COLS, :] = blocks[g]
        return c

    lax.fori_loop(0, PEERS, peer, 0, unroll=2)
    for c in copies:
        c.wait()


def start_values(ids, own, other, first, second):
    return pl.pallas_call(
        start_kernel,
        out_shape=(
            jax.ShapeDtypeStruct((COLS, OB * BLK), F32),
            pltpu.VMEM((PEERS, SLOTROWS, BLK), BF),
        ),
        in_specs=[VMEM] * 5,
        out_specs=[HBM, VMEM],
        scratch_shapes=[
            pltpu.VMEM((2, HALF, NB), BF),
            pltpu.VMEM((OB, COLS, BLK), BF),
            pltpu.VMEM((PIECES, COLS, PIECE), F32),
            pltpu.SMEM((PEERS, BLK), jnp.int32),
            pltpu.SemaphoreType.DMA((PIECES,)),
            pltpu.SemaphoreType.DMA,
        ],
        compiler_params=params(8),
        name="start_values",
    )(in_vmem(ids), in_vmem(own), in_vmem(other), in_vmem(first), in_vmem(second))


def resid_kernel(ids_v, received, scale, dual, resid, t0, t1, t2, t3, value, ids, sem, ids_sem):
    ids_copy = pltpu.make_async_copy(ids_v, ids, ids_sem)
    ids_copy.start()
    totals = (t0, t1, t2, t3)
    zero_totals(totals)
    weight = 1.0 / (1.0 + scale[...].astype(F32))
    ids_copy.wait()
    add_slots(received, ids, totals)
    copies = []
    for n in range(PIECES):
        for k in range(PIECE // BLK):
            b = n * (PIECE // BLK) + k
            value[n, :, k * BLK : (k + 1) * BLK] = (
                dual[b] - sum_totals(totals, b) * weight[b : b + 1, :]
            )
        copies.append(
            pltpu.make_async_copy(value.at[n], resid.at[:, pl.ds(n * PIECE, PIECE)], sem.at[n])
        )
        copies[n].start()
    for c in copies:
        c.wait()


def residual(ids, received, scale, dual):
    return pl.pallas_call(
        resid_kernel,
        out_shape=jax.ShapeDtypeStruct((COLS, OB * BLK), F32),
        in_specs=[VMEM] * 4,
        out_specs=HBM,
        scratch_shapes=TOTALS
        + [
            pltpu.VMEM((PIECES, COLS, PIECE), F32),
            pltpu.SMEM((PEERS, BLK), jnp.int32),
            pltpu.SemaphoreType.DMA((PIECES,)),
            pltpu.SemaphoreType.DMA,
        ],
        compiler_params=params(8),
        name="residual",
    )(in_vmem(ids), in_vmem(received), scale, in_vmem(dual))


def exchange(values):
    return lax.all_to_all(values, "sub", split_axis=0, concat_axis=0, tiled=True)


def per_device(loads, operators, owner, dual_block, scale_index, basis, coarse):
    scale = scale_index.reshape(OB, BLK)
    packed, pos, ops_v = first_apply(owner.reshape(NBLK), dual_block, loads, operators)
    received = exchange(packed)
    dual, keep, send, ids, coarse_v = project(received, scale, basis, coarse)
    own, other, first, second = sum_over_owners(keep, send, coarse_v, basis)
    start, requested = start_values(ids, own, other, first, second)
    again = second_apply(pos, exchange(requested), ops_v)
    return (start, residual(ids, exchange(again), scale, dual))


def solution(mesh):
    return jax.shard_map(
        per_device,
        mesh=mesh,
        in_specs=(
            P("sub", "rep", None),
            P("sub", None, None),
            P("sub", None),
            P("sub"),
            P("sub"),
            P("sub", None),
            P(),
        ),
        out_specs=(P("rep", "sub"), P("rep", "sub")),
        check_vma=False,
    )
```

```python
import functools

import jax
import jax.numpy as jnp
from jax import lax
from jax.experimental import pallas as pl
from jax.experimental.pallas import tpu as pltpu
from jax.sharding import PartitionSpec as P

BLK = 128
PEERS = 32
CAP = 4
COLS = 64
HALF = COLS // 2
L = 1024
BPS = 8
NSUB = 8
NBLK = NSUB * BPS
OB = 16
MERGE = OB * BLK // 2
NB = 1024
IDROWS = 8
SLOTROWS = CAP * COLS
BF = jnp.bfloat16
F32 = jnp.float32
HBM = pl.BlockSpec(memory_space=pl.ANY)
SMEM = pl.BlockSpec(memory_space=pltpu.SMEM)
VMEM = pl.BlockSpec(memory_space=pltpu.VMEM)
AHEAD = 4


def params(mib):
    return pltpu.CompilerParams(vmem_limit_bytes=mib * 1024 * 1024)


def in_hbm(x):
    return pltpu.with_memory_space_constraint(x, pltpu.HBM)


def in_vmem(x):
    return pltpu.with_memory_space_constraint(x, pltpu.VMEM)


def slot(ref, p):
    return ref.at[p // CAP, pl.ds(pl.multiple_of((p % CAP) * COLS, COLS), COLS)]


def first_kernel(owner_h, block_h, loads, ops, out, pos, ops_v, owner, dual_block, count, loads_v, sem, load_sem, idx_sem):
    owner_copy = pltpu.make_async_copy(owner_h, owner, idx_sem.at[0])
    block_copy = pltpu.make_async_copy(block_h, dual_block, idx_sem.at[1])
    owner_copy.start()
    block_copy.start()
    load_copy = pltpu.make_async_copy(loads, loads_v, load_sem)
    copies = [pltpu.make_async_copy(ops.at[s], ops_v.at[s], sem.at[s]) for s in range(NSUB)]
    load_copy.start()
    for s in range(AHEAD):
        copies[s].start()

    def zero(i, c):
        count[i] = 0
        return c

    lax.fori_loop(0, PEERS, zero, 0)
    owner_copy.wait()
    block_copy.wait()
    row = lax.broadcasted_iota(jnp.int32, (PEERS, BLK), 0)
    lane = lax.broadcasted_iota(jnp.int32, (PEERS, BLK), 1)
    flat = jnp.where(lane < CAP, row * CAP + lane, -1)

    def rank(i, ids):
        d = owner[i]
        r = count[d]
        count[d] = r + 1
        p = d * CAP + r
        pos[i] = p
        return jnp.where(flat == p, dual_block[i], ids)

    ids = lax.fori_loop(0, NBLK, rank, jnp.full((PEERS, BLK), -1, jnp.int32))
    out[:, SLOTROWS : SLOTROWS + IDROWS, :] = jnp.broadcast_to(
        ids.astype(F32)[:, None, :], (PEERS, IDROWS, BLK)
    ).astype(BF)
    load_copy.wait()
    for s in range(NSUB):
        copies[s].wait()
        if s + AHEAD < NSUB:
            copies[s + AHEAD].start()
        prod = jnp.dot(loads_v[s], ops_v[s], preferred_element_type=F32)
        for j in range(BPS):
            slot(out, pos[s * BPS + j])[...] = prod[:, j * BLK : (j + 1) * BLK].astype(BF)


def first_apply(owner, dual_block, loads, operators):
    return pl.pallas_call(
        first_kernel,
        out_shape=(
            pltpu.VMEM((PEERS, SLOTROWS + IDROWS, BLK), BF),
            jax.ShapeDtypeStruct((NBLK,), jnp.int32),
            pltpu.VMEM((NSUB, L, L), BF),
        ),
        in_specs=[HBM] * 4,
        out_specs=[VMEM, SMEM, VMEM],
        scratch_shapes=[
            pltpu.SMEM((NBLK,), jnp.int32),
            pltpu.SMEM((NBLK,), jnp.int32),
            pltpu.SMEM((PEERS,), jnp.int32),
            pltpu.VMEM((NSUB, COLS, L), BF),
            pltpu.SemaphoreType.DMA((NSUB,)),
            pltpu.SemaphoreType.DMA,
            pltpu.SemaphoreType.DMA((2,)),
        ],
        compiler_params=params(8),
        name="first_apply",
    )(in_hbm(owner), in_hbm(dual_block), in_hbm(loads), in_hbm(operators))


def second_kernel(pos, back, ops, out, local):
    for s in range(NSUB):
        for j in range(BPS):
            local[s, :, j * BLK : (j + 1) * BLK] = slot(back, pos[s * BPS + j])[...]
    for s in range(NSUB):
        prod = jnp.dot(local[s], ops[s], preferred_element_type=F32)
        for j in range(BPS):
            slot(out, pos[s * BPS + j])[...] = prod[:, j * BLK : (j + 1) * BLK].astype(BF)


def second_apply(pos, back, operators):
    return pl.pallas_call(
        second_kernel,
        out_shape=pltpu.VMEM((PEERS, SLOTROWS, BLK), BF),
        in_specs=[SMEM, VMEM, VMEM],
        out_specs=VMEM,
        scratch_shapes=[pltpu.VMEM((NSUB, COLS, L), BF)],
        compiler_params=params(8),
        name="second_apply",
    )(pos, in_vmem(back), in_vmem(operators))


def merge_kernel(part, coarse, basis, after, merged):
    for k in range(4):
        rows = slice(part * MERGE + k * 256, part * MERGE + (k + 1) * 256)
        merged[:, k * 256 : (k + 1) * 256] = lax.dot_general(
            coarse[...], basis[rows, :], (((1,), (1,)), ((), ())), preferred_element_type=F32
        ).astype(BF)


def merge(part, coarse, basis, after):
    return pl.pallas_call(
        functools.partial(merge_kernel, part),
        out_shape=pltpu.VMEM((NB, MERGE), BF),
        in_specs=[VMEM] * 3,
        out_specs=VMEM,
        compiler_params=params(6),
        name="merge",
    )(in_vmem(coarse), in_vmem(basis), in_vmem(after))


def zero_totals(totals):
    for q in range(CAP):
        totals[q][...] = jnp.zeros(totals[q].shape, F32)


def add_slots(received, ids, totals):
    def peer(p, c):
        for q in range(CAP):
            g = ids[p, q]
            g = jnp.where(g < 0, OB, g)
            totals[q][g] = totals[q][g] + received[p, q * COLS : (q + 1) * COLS, :].astype(F32)
        return c

    lax.fori_loop(0, PEERS, peer, 0, unroll=2)


def sum_totals(totals, b):
    return (totals[0][b] + totals[1][b]) + (totals[2][b] + totals[3][b])


TOTALS = [pltpu.VMEM((OB + 1, COLS, BLK), F32)] * CAP


def project_kernel(received, scale, basis, coarse, dual, keep, send, ids_out, coarse_v, t0, t1, t2, t3, narrow, coeff, idv, ids, sem, coarse_sem):
    coarse_copy = pltpu.make_async_copy(coarse, coarse_v, coarse_sem)
    coarse_copy.start()
    totals = (t0, t1, t2, t3)
    idv[...] = received[:, SLOTROWS : SLOTROWS + IDROWS, :].astype(F32)[:, 0, :].astype(jnp.int32)
    ids_copy = pltpu.make_async_copy(idv, ids, sem)
    ids_copy.start()
    ids_out[...] = idv[...]
    zero_totals(totals)
    ids_copy.wait()
    add_slots(received, ids, totals)
    weight = 1.0 / (1.0 + scale[...].astype(F32))
    for b in range(OB):
        owned = sum_totals(totals, b) * weight[b : b + 1, :]
        dual[b] = owned
        narrow[:, b * BLK : (b + 1) * BLK] = owned.astype(BF)
    product = jnp.dot(narrow[...], basis[...], preferred_element_type=F32)
    coeff[0] = product[:HALF]
    coeff[1] = product[HALF:]
    core = lax.axis_index("sub") % 2
    keep[...] = coeff[core]
    send[...] = coeff[1 - core]
    coarse_copy.wait()


def project(received, scale, basis, coarse):
    return pl.pallas_call(
        project_kernel,
        out_shape=(
            pltpu.VMEM((OB, COLS, BLK), F32),
            pltpu.VMEM((HALF, NB), F32),
            pltpu.VMEM((HALF, NB), F32),
            pltpu.VMEM((PEERS, BLK), jnp.int32),
            pltpu.VMEM((NB, NB), BF),
        ),
        in_specs=[VMEM] * 3 + [HBM],
        out_specs=[VMEM] * 5,
        scratch_shapes=TOTALS
        + [
            pltpu.VMEM((COLS, OB * BLK), BF),
            pltpu.VMEM((2, HALF, NB), F32),
            pltpu.VMEM((PEERS, BLK), jnp.int32),
            pltpu.SMEM((PEERS, BLK), jnp.int32),
            pltpu.SemaphoreType.DMA,
            pltpu.SemaphoreType.DMA,
        ],
        compiler_params=params(8),
        name="project",
    )(in_vmem(received), scale, in_vmem(basis), in_hbm(coarse))


def add_kernel(count, inputs, *refs):
    total = refs[0][...]
    for other in refs[1:count]:
        total = total + other[...].astype(F32)
    for out in refs[inputs:]:
        out[...] = total.astype(out.dtype)


def add_parts(own, others, types, after=()):
    count = 1 + len(others)
    inputs = count + len(after)
    return pl.pallas_call(
        functools.partial(add_kernel, count, inputs),
        out_shape=[pltpu.VMEM((HALF, NB), t) for t in types],
        in_specs=[VMEM] * inputs,
        out_specs=[VMEM] * len(types),
        compiler_params=params(4),
        name="add_parts",
    )(in_vmem(own), *[in_vmem(o) for o in (*others, *after)])


def swapped(values, kx, ky, kc):
    pairs = [(i, i ^ (kx * 8 + ky * 2 + kc)) for i in range(PEERS)]
    return lax.ppermute(values, "sub", pairs)


def sum_over_owners(keep, send, coarse, basis):
    both = (F32, BF)
    total, narrow = add_parts(keep, [swapped(send, 0, 0, 1)], both)
    first = merge(0, coarse, basis, narrow)
    others = [swapped(narrow, k, 0, 0) for k in (3, 1, 2)]
    total, narrow = add_parts(total, others, both, (first,))
    second = merge(1, coarse, basis, narrow)
    others = [swapped(narrow, 0, k, 0) for k in (3, 1, 2)]
    (narrow,) = add_parts(total, others, (BF,), (second,))
    return narrow, swapped(narrow, 0, 0, 1), first, second


PIECES = 4
PIECE = OB * BLK // PIECES


def start_kernel(ids_v, own, other, first, second, start, out, coeff, blocks, value, ids, sem, ids_sem):
    ids_copy = pltpu.make_async_copy(ids_v, ids, ids_sem)
    ids_copy.start()
    core = lax.axis_index("sub") % 2
    coeff[core] = own[...]
    coeff[1 - core] = other[...]
    copies = []
    for n in range(PIECES):
        merged = (first, second)[n // 2]
        cols = slice(n % 2 * PIECE, (n % 2 + 1) * PIECE)
        value[n] = jnp.dot(
            coeff[...].reshape(COLS, NB), merged[:, cols], preferred_element_type=F32
        )
        copies.append(
            pltpu.make_async_copy(value.at[n], start.at[:, pl.ds(n * PIECE, PIECE)], sem.at[n])
        )
        copies[n].start()
        for k in range(PIECE // BLK):
            blocks[n * (PIECE // BLK) + k] = value[n, :, k * BLK : (k + 1) * BLK].astype(BF)
    ids_copy.wait()

    def peer(p, c):
        for q in range(CAP):
            g = jnp.maximum(ids[p, q], 0)
            out[p, q * COLS : (q + 1) * COLS, :] = blocks[g]
        return c

    lax.fori_loop(0, PEERS, peer, 0, unroll=2)
    for c in copies:
        c.wait()


def start_values(ids, own, other, first, second):
    return pl.pallas_call(
        start_kernel,
        out_shape=(
            jax.ShapeDtypeStruct((COLS, OB * BLK), F32),
            pltpu.VMEM((PEERS, SLOTROWS, BLK), BF),
        ),
        in_specs=[VMEM] * 5,
        out_specs=[HBM, VMEM],
        scratch_shapes=[
            pltpu.VMEM((2, HALF, NB), BF),
            pltpu.VMEM((OB, COLS, BLK), BF),
            pltpu.VMEM((PIECES, COLS, PIECE), F32),
            pltpu.SMEM((PEERS, BLK), jnp.int32),
            pltpu.SemaphoreType.DMA((PIECES,)),
            pltpu.SemaphoreType.DMA,
        ],
        compiler_params=params(8),
        name="start_values",
    )(in_vmem(ids), in_vmem(own), in_vmem(other), in_vmem(first), in_vmem(second))


def resid_kernel(ids_v, received, scale, dual, resid, t0, t1, t2, t3, value, ids, sem, ids_sem):
    ids_copy = pltpu.make_async_copy(ids_v, ids, ids_sem)
    ids_copy.start()
    totals = (t0, t1, t2, t3)
    zero_totals(totals)
    weight = 1.0 / (1.0 + scale[...].astype(F32))
    ids_copy.wait()
    add_slots(received, ids, totals)
    copies = []
    for n in range(PIECES):
        for k in range(PIECE // BLK):
            b = n * (PIECE // BLK) + k
            value[n, :, k * BLK : (k + 1) * BLK] = (
                dual[b] - sum_totals(totals, b) * weight[b : b + 1, :]
            )
        copies.append(
            pltpu.make_async_copy(value.at[n], resid.at[:, pl.ds(n * PIECE, PIECE)], sem.at[n])
        )
        copies[n].start()
    for c in copies:
        c.wait()


def residual(ids, received, scale, dual):
    return pl.pallas_call(
        resid_kernel,
        out_shape=jax.ShapeDtypeStruct((COLS, OB * BLK), F32),
        in_specs=[VMEM] * 4,
        out_specs=HBM,
        scratch_shapes=TOTALS
        + [
            pltpu.VMEM((PIECES, COLS, PIECE), F32),
            pltpu.SMEM((PEERS, BLK), jnp.int32),
            pltpu.SemaphoreType.DMA((PIECES,)),
            pltpu.SemaphoreType.DMA,
        ],
        compiler_params=params(8),
        name="residual",
    )(in_vmem(ids), in_vmem(received), scale, in_vmem(dual))


def exchange(values):
    return lax.all_to_all(values, "sub", split_axis=0, concat_axis=0, tiled=True)


def per_device(loads, operators, owner, dual_block, scale_index, basis, coarse):
    scale = scale_index.reshape(OB, BLK)
    packed, pos, ops_v = first_apply(owner.reshape(NBLK), dual_block, loads, operators)
    received = exchange(packed)
    dual, keep, send, ids, coarse_v = project(received, scale, basis, coarse)
    own, other, first, second = sum_over_owners(keep, send, coarse_v, basis)
    start, requested = start_values(ids, own, other, first, second)
    again = second_apply(pos, exchange(requested), ops_v)
    return (start, residual(ids, exchange(again), scale, dual))


def solution(mesh):
    return jax.shard_map(
        per_device,
        mesh=mesh,
        in_specs=(
            P("sub", "rep", None),
            P("sub", None, None),
            P("sub", None),
            P("sub"),
            P("sub"),
            P("sub", None),
            P(),
        ),
        out_specs=(P("rep", "sub"), P("rep", "sub")),
        check_vma=False,
    )
```

```python
import functools

import jax
import jax.numpy as jnp
from jax import lax
from jax.experimental import pallas as pl
from jax.experimental.pallas import tpu as pltpu
from jax.sharding import PartitionSpec as P

BLK = 128
PEERS = 32
CAP = 4
COLS = 64
HALF = COLS // 2
L = 1024
BPS = 8
NSUB = 8
NBLK = NSUB * BPS
OB = 16
MERGE = OB * BLK // 2
NB = 1024
SLOTROWS = CAP * COLS
BF = jnp.bfloat16
F32 = jnp.float32
HBM = pl.BlockSpec(memory_space=pl.ANY)
SMEM = pl.BlockSpec(memory_space=pltpu.SMEM)
VMEM = pl.BlockSpec(memory_space=pltpu.VMEM)
AHEAD = 4


def params(mib):
    return pltpu.CompilerParams(vmem_limit_bytes=mib * 1024 * 1024)


def in_hbm(x):
    return pltpu.with_memory_space_constraint(x, pltpu.HBM)


def in_vmem(x):
    return pltpu.with_memory_space_constraint(x, pltpu.VMEM)


def slot(ref, p):
    return ref.at[p // CAP, pl.ds(pl.multiple_of((p % CAP) * COLS, COLS), COLS)]


def block_copy(blocks, out, pos, sem, i):
    return pltpu.make_async_copy(blocks.at[i], slot(out, pos[i]), sem.at[i])


def first_kernel(owner_h, block_h, loads, ops, out, pos, codes, owner, dual_block, count, loads_v, ops_v, blocks, sem, load_sem, idx_sem, out_sem):
    owner_copy = pltpu.make_async_copy(owner_h, owner, idx_sem.at[0])
    block_id_copy = pltpu.make_async_copy(block_h, dual_block, idx_sem.at[1])
    owner_copy.start()
    block_id_copy.start()
    load_copy = pltpu.make_async_copy(loads, loads_v, load_sem)
    copies = [pltpu.make_async_copy(ops.at[s], ops_v.at[s], sem.at[s]) for s in range(NSUB)]
    load_copy.start()
    for s in range(AHEAD):
        copies[s].start()

    def zero(i, c):
        count[i] = 0
        return c

    lax.fori_loop(0, PEERS, zero, 0)
    owner_copy.wait()
    block_id_copy.wait()
    lane = lax.broadcasted_iota(jnp.int32, (8, BLK), 1)

    def rank(i, ids):
        d = owner[i]
        r = count[d]
        count[d] = r + 1
        p = d * CAP + r
        pos[i] = p
        return jnp.where(lane == p, dual_block[i], ids)

    ids = lax.fori_loop(0, NBLK, rank, jnp.full((8, BLK), -1, jnp.int32))
    codes[...] = ids.astype(F32)
    load_copy.wait()
    for s in range(NSUB):
        copies[s].wait()
        if s + AHEAD < NSUB:
            copies[s + AHEAD].start()
        prod = jnp.dot(loads_v[s], ops_v[s], preferred_element_type=F32)
        for j in range(BPS):
            blocks[s * BPS + j] = prod[:, j * BLK : (j + 1) * BLK].astype(BF)
        for j in range(BPS):
            block_copy(blocks, out, pos, out_sem, s * BPS + j).start()

    def finish(i, c):
        block_copy(blocks, out, pos, out_sem, i).wait()
        return c

    lax.fori_loop(0, NBLK, finish, 0)


def first_apply(owner, dual_block, loads, operators):
    return pl.pallas_call(
        first_kernel,
        out_shape=(
            pltpu.HBM((PEERS, SLOTROWS, BLK), BF),
            jax.ShapeDtypeStruct((NBLK,), jnp.int32),
            jax.ShapeDtypeStruct((8, BLK), F32),
        ),
        in_specs=[HBM] * 4,
        out_specs=[HBM, SMEM, VMEM],
        scratch_shapes=[
            pltpu.SMEM((NBLK,), jnp.int32),
            pltpu.SMEM((NBLK,), jnp.int32),
            pltpu.SMEM((PEERS,), jnp.int32),
            pltpu.VMEM((NSUB, COLS, L), BF),
            pltpu.VMEM((NSUB, L, L), BF),
            pltpu.VMEM((NBLK, COLS, BLK), BF),
            pltpu.SemaphoreType.DMA((NSUB,)),
            pltpu.SemaphoreType.DMA,
            pltpu.SemaphoreType.DMA((2,)),
            pltpu.SemaphoreType.DMA((NBLK,)),
        ],
        compiler_params=params(26),
        name="first_apply",
    )(in_hbm(owner), in_hbm(dual_block), in_hbm(loads), in_hbm(operators))


def stack_kernel(*refs):
    for i, ref in enumerate(refs[:-1]):
        rows = ref.shape[0]
        refs[-1][i * rows : (i + 1) * rows] = ref[...]


def stack(parts):
    rows = len(parts) * parts[0].shape[0]
    return pl.pallas_call(
        stack_kernel,
        out_shape=jax.ShapeDtypeStruct((rows, BLK), F32),
        in_specs=[VMEM] * len(parts),
        out_specs=VMEM,
        compiler_params=params(2),
        name="stack",
    )(*parts)


def pick_kernel(*refs):
    me = lax.axis_index("sub")
    row = lax.broadcasted_iota(jnp.int32, (BLK, BLK), 0)
    lane = lax.broadcasted_iota(jnp.int32, (BLK, BLK), 1)
    chosen = jnp.where((row == me * CAP + lane) & (lane < CAP), 1.0, 0.0).astype(BF)
    for ky in range(4):
        picked = jnp.dot(refs[ky][...].astype(BF), chosen, preferred_element_type=F32)
        for kx in range(4):
            for kc in range(2):
                k = kx * 8 + ky * 2 + kc
                r = (kx * 2 + kc) * 8
                refs[4][k : k + 1, :] = picked[r : r + 1, :].astype(jnp.int32)


def gather_ids(codes):
    codes = stack([codes, swapped(codes, 0, 0, 1)])
    codes = stack([codes] + [swapped(codes, k, 0, 0) for k in (1, 2, 3)])
    return pl.pallas_call(
        pick_kernel,
        out_shape=jax.ShapeDtypeStruct((PEERS, BLK), jnp.int32),
        in_specs=[VMEM] * 4,
        out_specs=VMEM,
        compiler_params=params(2),
        name="pick",
    )(codes, *[swapped(codes, 0, k, 0) for k in (1, 2, 3)])


def second_kernel(pos, back, ops, out, local):
    for s in range(NSUB):
        for j in range(BPS):
            local[s, :, j * BLK : (j + 1) * BLK] = slot(back, pos[s * BPS + j])[...]
    for s in range(NSUB):
        prod = jnp.dot(local[s], ops[s], preferred_element_type=F32)
        for j in range(BPS):
            slot(out, pos[s * BPS + j])[...] = prod[:, j * BLK : (j + 1) * BLK].astype(BF)


def second_apply(pos, back, operators):
    return pl.pallas_call(
        second_kernel,
        out_shape=pltpu.VMEM((PEERS, SLOTROWS, BLK), BF),
        in_specs=[SMEM, VMEM, VMEM],
        out_specs=VMEM,
        scratch_shapes=[pltpu.VMEM((NSUB, COLS, L), BF)],
        compiler_params=params(8),
        name="second_apply",
    )(pos, in_vmem(back), in_vmem(operators))


def merge_kernel(part, coarse, basis, after, merged):
    for k in range(4):
        rows = slice(part * MERGE + k * 256, part * MERGE + (k + 1) * 256)
        merged[:, k * 256 : (k + 1) * 256] = lax.dot_general(
            coarse[...], basis[rows, :], (((1,), (1,)), ((), ())), preferred_element_type=F32
        ).astype(BF)


def merge(part, coarse, basis, after):
    return pl.pallas_call(
        functools.partial(merge_kernel, part),
        out_shape=pltpu.VMEM((NB, MERGE), BF),
        in_specs=[VMEM] * 3,
        out_specs=VMEM,
        compiler_params=params(6),
        name="merge",
    )(in_vmem(coarse), in_vmem(basis), in_vmem(after))


def zero_totals(totals):
    for q in range(CAP):
        totals[q][...] = jnp.zeros(totals[q].shape, F32)


def add_slots(received, ids, totals):
    me = lax.axis_index("sub")

    def peer(p, c):
        for q in range(CAP):
            g = ids[p ^ me, q]
            g = jnp.where(g < 0, OB, g)
            totals[q][g] = totals[q][g] + received[p, q * COLS : (q + 1) * COLS, :].astype(F32)
        return c

    lax.fori_loop(0, PEERS, peer, 0, unroll=2)


def sum_totals(totals, b):
    return (totals[0][b] + totals[1][b]) + (totals[2][b] + totals[3][b])


TOTALS = [pltpu.VMEM((OB + 1, COLS, BLK), F32)] * CAP


def project_kernel(ids_v, received, scale, basis, coarse, dual, keep, send, basis_v, coarse_v, t0, t1, t2, t3, narrow, coeff, ids, sem, basis_sem, coarse_sem):
    basis_copy = pltpu.make_async_copy(basis, basis_v, basis_sem)
    basis_copy.start()
    coarse_copy = pltpu.make_async_copy(coarse, coarse_v, coarse_sem)
    totals = (t0, t1, t2, t3)
    ids_copy = pltpu.make_async_copy(ids_v, ids, sem)
    ids_copy.start()
    zero_totals(totals)
    ids_copy.wait()
    add_slots(received, ids, totals)
    weight = 1.0 / (1.0 + scale[...].astype(F32))
    for b in range(OB):
        owned = sum_totals(totals, b) * weight[b : b + 1, :]
        dual[b] = owned
        narrow[:, b * BLK : (b + 1) * BLK] = owned.astype(BF)
    basis_copy.wait()
    coarse_copy.start()
    product = jnp.dot(narrow[...], basis_v[...], preferred_element_type=F32)
    coeff[0] = product[:HALF]
    coeff[1] = product[HALF:]
    core = lax.axis_index("sub") % 2
    keep[...] = coeff[core]
    send[...] = coeff[1 - core]
    coarse_copy.wait()


def project(ids, received, scale, basis, coarse):
    return pl.pallas_call(
        project_kernel,
        out_shape=(
            pltpu.VMEM((OB, COLS, BLK), F32),
            pltpu.VMEM((HALF, NB), F32),
            pltpu.VMEM((HALF, NB), F32),
            pltpu.VMEM((OB * BLK, NB), BF),
            pltpu.VMEM((NB, NB), BF),
        ),
        in_specs=[VMEM] * 3 + [HBM] * 2,
        out_specs=[VMEM] * 5,
        scratch_shapes=TOTALS
        + [
            pltpu.VMEM((COLS, OB * BLK), BF),
            pltpu.VMEM((2, HALF, NB), F32),
            pltpu.SMEM((PEERS, BLK), jnp.int32),
            pltpu.SemaphoreType.DMA,
            pltpu.SemaphoreType.DMA,
            pltpu.SemaphoreType.DMA,
        ],
        compiler_params=params(8),
        name="project",
    )(in_vmem(ids), in_vmem(received), scale, in_hbm(basis), in_hbm(coarse))


def add_kernel(count, inputs, *refs):
    total = refs[0][...]
    for other in refs[1:count]:
        total = total + other[...].astype(F32)
    for out in refs[inputs:]:
        out[...] = total.astype(out.dtype)


def add_parts(own, others, types, after=()):
    count = 1 + len(others)
    inputs = count + len(after)
    return pl.pallas_call(
        functools.partial(add_kernel, count, inputs),
        out_shape=[pltpu.VMEM((HALF, NB), t) for t in types],
        in_specs=[VMEM] * inputs,
        out_specs=[VMEM] * len(types),
        compiler_params=params(4),
        name="add_parts",
    )(in_vmem(own), *[in_vmem(o) for o in (*others, *after)])


def swapped(values, kx, ky, kc):
    pairs = [(i, i ^ (kx * 8 + ky * 2 + kc)) for i in range(PEERS)]
    return lax.ppermute(values, "sub", pairs)


def sum_over_owners(keep, send, coarse, basis):
    both = (F32, BF)
    total, narrow = add_parts(keep, [swapped(send, 0, 0, 1)], both)
    first = merge(0, coarse, basis, narrow)
    others = [swapped(narrow, k, 0, 0) for k in (3, 1, 2)]
    total, narrow = add_parts(total, others, both, (first,))
    second = merge(1, coarse, basis, narrow)
    others = [swapped(narrow, 0, k, 0) for k in (3, 1, 2)]
    (narrow,) = add_parts(total, others, (BF,), (second,))
    return narrow, swapped(narrow, 0, 0, 1), first, second


PIECES = 4
PIECE = OB * BLK // PIECES


def start_kernel(ids_v, own, other, first, second, start, out, coeff, blocks, value, ids, sem, ids_sem):
    ids_copy = pltpu.make_async_copy(ids_v, ids, ids_sem)
    ids_copy.start()
    me = lax.axis_index("sub")
    core = me % 2
    coeff[core] = own[...]
    coeff[1 - core] = other[...]
    copies = []
    for n in range(PIECES):
        merged = (first, second)[n // 2]
        cols = slice(n % 2 * PIECE, (n % 2 + 1) * PIECE)
        value[n] = jnp.dot(
            coeff[...].reshape(COLS, NB), merged[:, cols], preferred_element_type=F32
        )
        copies.append(
            pltpu.make_async_copy(value.at[n], start.at[:, pl.ds(n * PIECE, PIECE)], sem.at[n])
        )
        copies[n].start()
        for k in range(PIECE // BLK):
            blocks[n * (PIECE // BLK) + k] = value[n, :, k * BLK : (k + 1) * BLK].astype(BF)
    ids_copy.wait()

    def peer(p, c):
        for q in range(CAP):
            g = jnp.maximum(ids[p ^ me, q], 0)
            out[p, q * COLS : (q + 1) * COLS, :] = blocks[g]
        return c

    lax.fori_loop(0, PEERS, peer, 0, unroll=2)
    for c in copies:
        c.wait()


def start_values(ids, own, other, first, second):
    return pl.pallas_call(
        start_kernel,
        out_shape=(
            jax.ShapeDtypeStruct((COLS, OB * BLK), F32),
            pltpu.VMEM((PEERS, SLOTROWS, BLK), BF),
        ),
        in_specs=[VMEM] * 5,
        out_specs=[HBM, VMEM],
        scratch_shapes=[
            pltpu.VMEM((2, HALF, NB), BF),
            pltpu.VMEM((OB, COLS, BLK), BF),
            pltpu.VMEM((PIECES, COLS, PIECE), F32),
            pltpu.SMEM((PEERS, BLK), jnp.int32),
            pltpu.SemaphoreType.DMA((PIECES,)),
            pltpu.SemaphoreType.DMA,
        ],
        compiler_params=params(8),
        name="start_values",
    )(in_vmem(ids), in_vmem(own), in_vmem(other), in_vmem(first), in_vmem(second))


def resid_kernel(ids_v, received, scale, dual, resid, t0, t1, t2, t3, value, ids, sem, ids_sem):
    ids_copy = pltpu.make_async_copy(ids_v, ids, ids_sem)
    ids_copy.start()
    totals = (t0, t1, t2, t3)
    zero_totals(totals)
    weight = 1.0 / (1.0 + scale[...].astype(F32))
    ids_copy.wait()
    add_slots(received, ids, totals)
    copies = []
    for n in range(PIECES):
        for k in range(PIECE // BLK):
            b = n * (PIECE // BLK) + k
            value[n, :, k * BLK : (k + 1) * BLK] = (
                dual[b] - sum_totals(totals, b) * weight[b : b + 1, :]
            )
        copies.append(
            pltpu.make_async_copy(value.at[n], resid.at[:, pl.ds(n * PIECE, PIECE)], sem.at[n])
        )
        copies[n].start()
    for c in copies:
        c.wait()


def residual(ids, received, scale, dual):
    return pl.pallas_call(
        resid_kernel,
        out_shape=jax.ShapeDtypeStruct((COLS, OB * BLK), F32),
        in_specs=[VMEM] * 4,
        out_specs=HBM,
        scratch_shapes=TOTALS
        + [
            pltpu.VMEM((PIECES, COLS, PIECE), F32),
            pltpu.SMEM((PEERS, BLK), jnp.int32),
            pltpu.SemaphoreType.DMA((PIECES,)),
            pltpu.SemaphoreType.DMA,
        ],
        compiler_params=params(8),
        name="residual",
    )(in_vmem(ids), in_vmem(received), scale, in_vmem(dual))


def exchange(values):
    return lax.all_to_all(values, "sub", split_axis=0, concat_axis=0, tiled=True)


def per_device(loads, operators, owner, dual_block, scale_index, basis, coarse):
    scale = scale_index.reshape(OB, BLK)
    packed, pos, codes = first_apply(owner.reshape(NBLK), dual_block, loads, operators)
    ids = gather_ids(codes)
    received = exchange(packed)
    dual, keep, send, basis_v, coarse_v = project(ids, received, scale, basis, coarse)
    own, other, first, second = sum_over_owners(keep, send, coarse_v, basis_v)
    start, requested = start_values(ids, own, other, first, second)
    again = second_apply(pos, exchange(requested), operators)
    return (start, residual(ids, exchange(again), scale, dual))


def solution(mesh):
    return jax.shard_map(
        per_device,
        mesh=mesh,
        in_specs=(
            P("sub", "rep", None),
            P("sub", None, None),
            P("sub", None),
            P("sub"),
            P("sub"),
            P("sub", None),
            P(),
        ),
        out_specs=(P("rep", "sub"), P("rep", "sub")),
        check_vma=False,
    )
```

```python
import functools

import jax
import jax.numpy as jnp
from jax import lax
from jax.experimental import pallas as pl
from jax.experimental.pallas import tpu as pltpu
from jax.sharding import PartitionSpec as P

BLK = 128
PEERS = 32
CAP = 4
COLS = 64
HALF = COLS // 2
L = 1024
BPS = 8
NSUB = 8
NBLK = NSUB * BPS
OB = 16
MERGE = OB * BLK // 2
NB = 1024
IDROWS = 8
SLOTROWS = CAP * COLS
BF = jnp.bfloat16
F32 = jnp.float32
HBM = pl.BlockSpec(memory_space=pl.ANY)
SMEM = pl.BlockSpec(memory_space=pltpu.SMEM)
VMEM = pl.BlockSpec(memory_space=pltpu.VMEM)
AHEAD = 5


def params(mib):
    return pltpu.CompilerParams(vmem_limit_bytes=mib * 1024 * 1024)


def in_hbm(x):
    return pltpu.with_memory_space_constraint(x, pltpu.HBM)


def in_vmem(x):
    return pltpu.with_memory_space_constraint(x, pltpu.VMEM)


def slot(ref, p):
    return ref.at[p // CAP, pl.ds(pl.multiple_of((p % CAP) * COLS, COLS), COLS)]


def first_kernel(owner_h, block_h, loads, ops, out, pos, ops_v, owner, dual_block, count, loads_v, sem, load_sem, idx_sem):
    owner_copy = pltpu.make_async_copy(owner_h, owner, idx_sem.at[0])
    block_copy = pltpu.make_async_copy(block_h, dual_block, idx_sem.at[1])
    owner_copy.start()
    block_copy.start()
    load_copies = [
        pltpu.make_async_copy(loads.at[s], loads_v.at[s], load_sem.at[s]) for s in range(NSUB)
    ]
    copies = [pltpu.make_async_copy(ops.at[s], ops_v.at[s], sem.at[s]) for s in range(NSUB)]
    for s in range(AHEAD):
        load_copies[s].start()
        copies[s].start()

    def zero(i, c):
        count[i] = 0
        return c

    lax.fori_loop(0, PEERS, zero, 0)
    owner_copy.wait()
    block_copy.wait()
    row = lax.broadcasted_iota(jnp.int32, (PEERS, BLK), 0)
    lane = lax.broadcasted_iota(jnp.int32, (PEERS, BLK), 1)
    flat = jnp.where(lane < CAP, row * CAP + lane, -1)

    def rank(i, ids):
        d = owner[i]
        r = count[d]
        count[d] = r + 1
        p = d * CAP + r
        pos[i] = p
        return jnp.where(flat == p, dual_block[i], ids)

    ids = lax.fori_loop(0, NBLK, rank, jnp.full((PEERS, BLK), -1, jnp.int32))
    out[:, SLOTROWS : SLOTROWS + IDROWS, :] = jnp.broadcast_to(
        ids.astype(F32)[:, None, :], (PEERS, IDROWS, BLK)
    ).astype(BF)
    for s in range(NSUB):
        load_copies[s].wait()
        copies[s].wait()
        if s + AHEAD < NSUB:
            load_copies[s + AHEAD].start()
            copies[s + AHEAD].start()
        prod = jnp.dot(loads_v[s], ops_v[s], preferred_element_type=F32)
        for j in range(BPS):
            slot(out, pos[s * BPS + j])[...] = prod[:, j * BLK : (j + 1) * BLK].astype(BF)


def first_apply(owner, dual_block, loads, operators):
    return pl.pallas_call(
        first_kernel,
        out_shape=(
            pltpu.VMEM((PEERS, SLOTROWS + IDROWS, BLK), BF),
            jax.ShapeDtypeStruct((NBLK,), jnp.int32),
            pltpu.VMEM((NSUB, L, L), BF),
        ),
        in_specs=[HBM] * 4,
        out_specs=[VMEM, SMEM, VMEM],
        scratch_shapes=[
            pltpu.SMEM((NBLK,), jnp.int32),
            pltpu.SMEM((NBLK,), jnp.int32),
            pltpu.SMEM((PEERS,), jnp.int32),
            pltpu.VMEM((NSUB, COLS, L), BF),
            pltpu.SemaphoreType.DMA((NSUB,)),
            pltpu.SemaphoreType.DMA((NSUB,)),
            pltpu.SemaphoreType.DMA((2,)),
        ],
        compiler_params=params(8),
        name="first_apply",
    )(in_hbm(owner), in_hbm(dual_block), in_hbm(loads), in_hbm(operators))


def second_kernel(pos, back, ops, out):
    for s in range(NSUB):
        local = jnp.concatenate([slot(back, pos[s * BPS + j])[...] for j in range(BPS)], axis=1)
        prod = jnp.dot(local, ops[s], preferred_element_type=F32)
        for j in range(BPS):
            slot(out, pos[s * BPS + j])[...] = prod[:, j * BLK : (j + 1) * BLK].astype(BF)


def second_apply(pos, back, operators):
    return pl.pallas_call(
        second_kernel,
        out_shape=pltpu.VMEM((PEERS, SLOTROWS, BLK), BF),
        in_specs=[SMEM, VMEM, VMEM],
        out_specs=VMEM,
        compiler_params=params(8),
        name="second_apply",
    )(pos, in_vmem(back), in_vmem(operators))


def merge_kernel(part, coarse, basis, after, merged):
    for k in range(4):
        rows = slice(part * MERGE + k * 256, part * MERGE + (k + 1) * 256)
        merged[:, k * 256 : (k + 1) * 256] = lax.dot_general(
            coarse[...], basis[rows, :], (((1,), (1,)), ((), ())), preferred_element_type=F32
        ).astype(BF)


def merge(part, coarse, basis, after):
    return pl.pallas_call(
        functools.partial(merge_kernel, part),
        out_shape=pltpu.VMEM((NB, MERGE), BF),
        in_specs=[VMEM] * 3,
        out_specs=VMEM,
        compiler_params=params(6),
        name="merge",
    )(in_vmem(coarse), in_vmem(basis), in_vmem(after))


def zero_totals(totals):
    for q in range(CAP):
        totals[q][...] = jnp.zeros(totals[q].shape, F32)


def add_slots(received, ids, totals):
    def peer(p, c):
        for q in range(CAP):
            g = ids[p, q]
            g = jnp.where(g < 0, OB, g)
            totals[q][g] = totals[q][g] + received[p, q * COLS : (q + 1) * COLS, :].astype(F32)
        return c

    lax.fori_loop(0, PEERS, peer, 0, unroll=2)


def sum_totals(totals, b):
    return (totals[0][b] + totals[1][b]) + (totals[2][b] + totals[3][b])


TOTALS = [pltpu.VMEM((OB + 1, COLS, BLK), F32)] * CAP


def project_kernel(received, scale, basis, coarse, dual, keep, send, ids_out, coarse_v, t0, t1, t2, t3, narrow, coeff, idv, ids, sem, coarse_sem):
    coarse_copy = pltpu.make_async_copy(coarse, coarse_v, coarse_sem)
    coarse_copy.start()
    totals = (t0, t1, t2, t3)
    idv[...] = received[:, SLOTROWS : SLOTROWS + IDROWS, :].astype(F32)[:, 0, :].astype(jnp.int32)
    ids_copy = pltpu.make_async_copy(idv, ids, sem)
    ids_copy.start()
    ids_out[...] = idv[...]
    zero_totals(totals)
    ids_copy.wait()
    add_slots(received, ids, totals)
    weight = 1.0 / (1.0 + scale[...].astype(F32))
    for b in range(OB):
        owned = sum_totals(totals, b) * weight[b : b + 1, :]
        dual[b] = owned
        narrow[:, b * BLK : (b + 1) * BLK] = owned.astype(BF)
    product = jnp.dot(narrow[...], basis[...], preferred_element_type=F32)
    coeff[0] = product[:HALF]
    coeff[1] = product[HALF:]
    core = lax.axis_index("sub") % 2
    keep[...] = coeff[core]
    send[...] = coeff[1 - core]
    coarse_copy.wait()


def project(received, scale, basis, coarse):
    return pl.pallas_call(
        project_kernel,
        out_shape=(
            pltpu.VMEM((OB, COLS, BLK), F32),
            pltpu.VMEM((HALF, NB), F32),
            pltpu.VMEM((HALF, NB), F32),
            pltpu.VMEM((PEERS, BLK), jnp.int32),
            pltpu.VMEM((NB, NB), BF),
        ),
        in_specs=[VMEM] * 3 + [HBM],
        out_specs=[VMEM] * 5,
        scratch_shapes=TOTALS
        + [
            pltpu.VMEM((COLS, OB * BLK), BF),
            pltpu.VMEM((2, HALF, NB), F32),
            pltpu.VMEM((PEERS, BLK), jnp.int32),
            pltpu.SMEM((PEERS, BLK), jnp.int32),
            pltpu.SemaphoreType.DMA,
            pltpu.SemaphoreType.DMA,
        ],
        compiler_params=params(8),
        name="project",
    )(in_vmem(received), scale, in_vmem(basis), in_hbm(coarse))


def add_kernel(count, inputs, *refs):
    total = refs[0][...]
    for other in refs[1:count]:
        total = total + other[...].astype(F32)
    for out in refs[inputs:]:
        out[...] = total.astype(out.dtype)


def add_parts(own, others, types, after=()):
    count = 1 + len(others)
    inputs = count + len(after)
    return pl.pallas_call(
        functools.partial(add_kernel, count, inputs),
        out_shape=[pltpu.VMEM((HALF, NB), t) for t in types],
        in_specs=[VMEM] * inputs,
        out_specs=[VMEM] * len(types),
        compiler_params=params(4),
        name="add_parts",
    )(in_vmem(own), *[in_vmem(o) for o in (*others, *after)])


def swapped(values, kx, ky, kc):
    pairs = [(i, i ^ (kx * 8 + ky * 2 + kc)) for i in range(PEERS)]
    return lax.ppermute(values, "sub", pairs)


def sum_over_owners(keep, send, coarse, basis):
    both = (F32, BF)
    total, narrow = add_parts(keep, [swapped(send, 0, 0, 1)], both)
    first = merge(0, coarse, basis, narrow)
    others = [swapped(narrow, k, 0, 0) for k in (3, 1, 2)]
    total, narrow = add_parts(total, others, both, (first,))
    second = merge(1, coarse, basis, narrow)
    others = [swapped(narrow, 0, k, 0) for k in (3, 1, 2)]
    (narrow,) = add_parts(total, others, (BF,), (second,))
    return narrow, swapped(narrow, 0, 0, 1), first, second


PIECES = 4
PIECE = OB * BLK // PIECES


def start_kernel(ids_v, own, other, first, second, start, out, coeff, blocks, value, ids, sem, ids_sem):
    ids_copy = pltpu.make_async_copy(ids_v, ids, ids_sem)
    ids_copy.start()
    core = lax.axis_index("sub") % 2
    coeff[core] = own[...]
    coeff[1 - core] = other[...]
    copies = []
    for n in range(PIECES):
        merged = (first, second)[n // 2]
        cols = slice(n % 2 * PIECE, (n % 2 + 1) * PIECE)
        value[n] = jnp.dot(
            coeff[...].reshape(COLS, NB), merged[:, cols], preferred_element_type=F32
        )
        copies.append(
            pltpu.make_async_copy(value.at[n], start.at[:, pl.ds(n * PIECE, PIECE)], sem.at[n])
        )
        copies[n].start()
        for k in range(PIECE // BLK):
            blocks[n * (PIECE // BLK) + k] = value[n, :, k * BLK : (k + 1) * BLK].astype(BF)
    ids_copy.wait()

    def peer(p, c):
        for q in range(CAP):
            g = jnp.maximum(ids[p, q], 0)
            out[p, q * COLS : (q + 1) * COLS, :] = blocks[g]
        return c

    lax.fori_loop(0, PEERS, peer, 0, unroll=2)
    for c in copies:
        c.wait()


def start_values(ids, own, other, first, second):
    return pl.pallas_call(
        start_kernel,
        out_shape=(
            jax.ShapeDtypeStruct((COLS, OB * BLK), F32),
            pltpu.VMEM((PEERS, SLOTROWS, BLK), BF),
        ),
        in_specs=[VMEM] * 5,
        out_specs=[HBM, VMEM],
        scratch_shapes=[
            pltpu.VMEM((2, HALF, NB), BF),
            pltpu.VMEM((OB, COLS, BLK), BF),
            pltpu.VMEM((PIECES, COLS, PIECE), F32),
            pltpu.SMEM((PEERS, BLK), jnp.int32),
            pltpu.SemaphoreType.DMA((PIECES,)),
            pltpu.SemaphoreType.DMA,
        ],
        compiler_params=params(8),
        name="start_values",
    )(in_vmem(ids), in_vmem(own), in_vmem(other), in_vmem(first), in_vmem(second))


def resid_kernel(ids_v, received, scale, dual, resid, t0, t1, t2, t3, value, ids, sem, ids_sem):
    ids_copy = pltpu.make_async_copy(ids_v, ids, ids_sem)
    ids_copy.start()
    totals = (t0, t1, t2, t3)
    zero_totals(totals)
    weight = 1.0 / (1.0 + scale[...].astype(F32))
    ids_copy.wait()
    add_slots(received, ids, totals)
    copies = []
    for n in range(PIECES):
        for k in range(PIECE // BLK):
            b = n * (PIECE // BLK) + k
            value[n, :, k * BLK : (k + 1) * BLK] = (
                dual[b] - sum_totals(totals, b) * weight[b : b + 1, :]
            )
        copies.append(
            pltpu.make_async_copy(value.at[n], resid.at[:, pl.ds(n * PIECE, PIECE)], sem.at[n])
        )
        copies[n].start()
    for c in copies:
        c.wait()


def residual(ids, received, scale, dual):
    return pl.pallas_call(
        resid_kernel,
        out_shape=jax.ShapeDtypeStruct((COLS, OB * BLK), F32),
        in_specs=[VMEM] * 4,
        out_specs=HBM,
        scratch_shapes=TOTALS
        + [
            pltpu.VMEM((PIECES, COLS, PIECE), F32),
            pltpu.SMEM((PEERS, BLK), jnp.int32),
            pltpu.SemaphoreType.DMA((PIECES,)),
            pltpu.SemaphoreType.DMA,
        ],
        compiler_params=params(8),
        name="residual",
    )(in_vmem(ids), in_vmem(received), scale, in_vmem(dual))


def exchange(values):
    return lax.all_to_all(values, "sub", split_axis=0, concat_axis=0, tiled=True)


def per_device(loads, operators, owner, dual_block, scale_index, basis, coarse):
    scale = scale_index.reshape(OB, BLK)
    packed, pos, ops_v = first_apply(owner.reshape(NBLK), dual_block, loads, operators)
    received = exchange(packed)
    dual, keep, send, ids, coarse_v = project(received, scale, basis, coarse)
    own, other, first, second = sum_over_owners(keep, send, coarse_v, basis)
    start, requested = start_values(ids, own, other, first, second)
    again = second_apply(pos, exchange(requested), ops_v)
    return (start, residual(ids, exchange(again), scale, dual))


def solution(mesh):
    return jax.shard_map(
        per_device,
        mesh=mesh,
        in_specs=(
            P("sub", "rep", None),
            P("sub", None, None),
            P("sub", None),
            P("sub"),
            P("sub"),
            P("sub", None),
            P(),
        ),
        out_specs=(P("rep", "sub"), P("rep", "sub")),
        check_vma=False,
    )
```

```python
import functools

import jax
import jax.numpy as jnp
from jax import lax
from jax.experimental import pallas as pl
from jax.experimental.pallas import tpu as pltpu
from jax.sharding import PartitionSpec as P

BLK = 128
PEERS = 32
CAP = 4
COLS = 64
HALF = COLS // 2
L = 1024
BPS = 8
NSUB = 8
NBLK = NSUB * BPS
OB = 16
MERGE = OB * BLK // 2
NB = 1024
IDROWS = 8
SLOTROWS = CAP * COLS
BF = jnp.bfloat16
F32 = jnp.float32
HBM = pl.BlockSpec(memory_space=pl.ANY)
SMEM = pl.BlockSpec(memory_space=pltpu.SMEM)
VMEM = pl.BlockSpec(memory_space=pltpu.VMEM)
AHEAD = 5


def params(mib):
    return pltpu.CompilerParams(vmem_limit_bytes=mib * 1024 * 1024)


def in_hbm(x):
    return pltpu.with_memory_space_constraint(x, pltpu.HBM)


def in_vmem(x):
    return pltpu.with_memory_space_constraint(x, pltpu.VMEM)


def slot(ref, p):
    return ref.at[p // CAP, pl.ds(pl.multiple_of((p % CAP) * COLS, COLS), COLS)]


def first_kernel(owner_h, block_h, loads, ops, out, pos, ops_v, owner, dual_block, count, loads_v, sem, load_sem, idx_sem):
    owner_copy = pltpu.make_async_copy(owner_h, owner, idx_sem.at[0])
    block_copy = pltpu.make_async_copy(block_h, dual_block, idx_sem.at[1])
    owner_copy.start()
    block_copy.start()
    load_copies = [
        pltpu.make_async_copy(loads.at[s], loads_v.at[s], load_sem.at[s]) for s in range(NSUB)
    ]
    copies = [pltpu.make_async_copy(ops.at[s], ops_v.at[s], sem.at[s]) for s in range(NSUB)]
    for s in range(AHEAD):
        load_copies[s].start()
        copies[s].start()

    def zero(i, c):
        count[i] = 0
        return c

    lax.fori_loop(0, PEERS, zero, 0)
    owner_copy.wait()
    block_copy.wait()
    row = lax.broadcasted_iota(jnp.int32, (PEERS, BLK), 0)
    lane = lax.broadcasted_iota(jnp.int32, (PEERS, BLK), 1)
    flat = jnp.where(lane < CAP, row * CAP + lane, -1)

    def rank(i, ids):
        d = owner[i]
        r = count[d]
        count[d] = r + 1
        p = d * CAP + r
        pos[i] = p
        return jnp.where(flat == p, dual_block[i], ids)

    ids = lax.fori_loop(0, NBLK, rank, jnp.full((PEERS, BLK), -1, jnp.int32))
    out[:, SLOTROWS : SLOTROWS + IDROWS, :] = jnp.broadcast_to(
        ids.astype(F32)[:, None, :], (PEERS, IDROWS, BLK)
    ).astype(BF)
    for s in range(NSUB):
        load_copies[s].wait()
        copies[s].wait()
        if s + AHEAD < NSUB:
            load_copies[s + AHEAD].start()
            copies[s + AHEAD].start()
        prod = jnp.dot(loads_v[s], ops_v[s], preferred_element_type=F32)
        for j in range(BPS):
            slot(out, pos[s * BPS + j])[...] = prod[:, j * BLK : (j + 1) * BLK].astype(BF)


def first_apply(owner, dual_block, loads, operators):
    return pl.pallas_call(
        first_kernel,
        out_shape=(
            pltpu.VMEM((PEERS, SLOTROWS + IDROWS, BLK), BF),
            jax.ShapeDtypeStruct((NBLK,), jnp.int32),
            pltpu.VMEM((NSUB, L, L), BF),
        ),
        in_specs=[HBM] * 4,
        out_specs=[VMEM, SMEM, VMEM],
        scratch_shapes=[
            pltpu.SMEM((NBLK,), jnp.int32),
            pltpu.SMEM((NBLK,), jnp.int32),
            pltpu.SMEM((PEERS,), jnp.int32),
            pltpu.VMEM((NSUB, COLS, L), BF),
            pltpu.SemaphoreType.DMA((NSUB,)),
            pltpu.SemaphoreType.DMA((NSUB,)),
            pltpu.SemaphoreType.DMA((2,)),
        ],
        compiler_params=params(8),
        name="first_apply",
    )(in_hbm(owner), in_hbm(dual_block), in_hbm(loads), in_hbm(operators))


def second_kernel(pos, back, ops, out):
    for s in range(NSUB):
        local = jnp.concatenate([slot(back, pos[s * BPS + j])[...] for j in range(BPS)], axis=1)
        prod = jnp.dot(local, ops[s], preferred_element_type=F32)
        for j in range(BPS):
            slot(out, pos[s * BPS + j])[...] = prod[:, j * BLK : (j + 1) * BLK].astype(BF)


def second_apply(pos, back, operators):
    return pl.pallas_call(
        second_kernel,
        out_shape=pltpu.VMEM((PEERS, SLOTROWS, BLK), BF),
        in_specs=[SMEM, VMEM, VMEM],
        out_specs=VMEM,
        compiler_params=params(8),
        name="second_apply",
    )(pos, in_vmem(back), in_vmem(operators))


def merge_kernel(part, coarse, basis, after, merged):
    for k in range(4):
        rows = slice(part * MERGE + k * 256, part * MERGE + (k + 1) * 256)
        merged[:, k * 256 : (k + 1) * 256] = lax.dot_general(
            coarse[...], basis[rows, :], (((1,), (1,)), ((), ())), preferred_element_type=F32
        ).astype(BF)


def merge(part, coarse, basis, after):
    return pl.pallas_call(
        functools.partial(merge_kernel, part),
        out_shape=pltpu.VMEM((NB, MERGE), BF),
        in_specs=[VMEM] * 3,
        out_specs=VMEM,
        compiler_params=params(6),
        name="merge",
    )(in_vmem(coarse), in_vmem(basis), in_vmem(after))


def zero_totals(totals):
    for q in range(CAP):
        totals[q][...] = jnp.zeros(totals[q].shape, F32)


def add_slots(received, ids, totals):
    def peer(p, c):
        for q in range(CAP):
            g = ids[p, q]
            g = jnp.where(g < 0, OB, g)
            totals[q][g] = totals[q][g] + received[p, q * COLS : (q + 1) * COLS, :].astype(F32)
        return c

    lax.fori_loop(0, PEERS, peer, 0, unroll=2)


def sum_totals(totals, b):
    return (totals[0][b] + totals[1][b]) + (totals[2][b] + totals[3][b])


TOTALS = [pltpu.VMEM((OB + 1, COLS, BLK), F32)] * CAP


def project_kernel(received, scale, basis, coarse, dual, keep, send, ids_out, coarse_v, t0, t1, t2, t3, narrow, coeff, idv, ids, sem, coarse_sem):
    coarse_copy = pltpu.make_async_copy(coarse, coarse_v, coarse_sem)
    coarse_copy.start()
    totals = (t0, t1, t2, t3)
    idv[...] = received[:, SLOTROWS : SLOTROWS + IDROWS, :].astype(F32)[:, 0, :].astype(jnp.int32)
    ids_copy = pltpu.make_async_copy(idv, ids, sem)
    ids_copy.start()
    ids_out[...] = idv[...]
    zero_totals(totals)
    ids_copy.wait()
    add_slots(received, ids, totals)
    weight = 1.0 / (1.0 + scale[...].astype(F32))
    for b in range(OB):
        owned = sum_totals(totals, b) * weight[b : b + 1, :]
        dual[b] = owned
        narrow[:, b * BLK : (b + 1) * BLK] = owned.astype(BF)
    product = jnp.dot(narrow[...], basis[...], preferred_element_type=F32)
    coeff[0] = product[:HALF]
    coeff[1] = product[HALF:]
    core = lax.axis_index("sub") % 2
    keep[...] = coeff[core]
    send[...] = coeff[1 - core]
    coarse_copy.wait()


def project(received, scale, basis, coarse):
    return pl.pallas_call(
        project_kernel,
        out_shape=(
            pltpu.VMEM((OB, COLS, BLK), F32),
            pltpu.VMEM((HALF, NB), F32),
            pltpu.VMEM((HALF, NB), F32),
            pltpu.VMEM((PEERS, BLK), jnp.int32),
            pltpu.VMEM((NB, NB), BF),
        ),
        in_specs=[VMEM] * 3 + [HBM],
        out_specs=[VMEM] * 5,
        scratch_shapes=TOTALS
        + [
            pltpu.VMEM((COLS, OB * BLK), BF),
            pltpu.VMEM((2, HALF, NB), F32),
            pltpu.VMEM((PEERS, BLK), jnp.int32),
            pltpu.SMEM((PEERS, BLK), jnp.int32),
            pltpu.SemaphoreType.DMA,
            pltpu.SemaphoreType.DMA,
        ],
        compiler_params=params(8),
        name="project",
    )(in_vmem(received), scale, in_vmem(basis), in_hbm(coarse))


def add_kernel(count, inputs, *refs):
    total = refs[0][...]
    for other in refs[1:count]:
        total = total + other[...].astype(F32)
    for out in refs[inputs:]:
        out[...] = total.astype(out.dtype)


def add_parts(own, others, types, after=()):
    count = 1 + len(others)
    inputs = count + len(after)
    return pl.pallas_call(
        functools.partial(add_kernel, count, inputs),
        out_shape=[pltpu.VMEM((HALF, NB), t) for t in types],
        in_specs=[VMEM] * inputs,
        out_specs=[VMEM] * len(types),
        compiler_params=params(4),
        name="add_parts",
    )(in_vmem(own), *[in_vmem(o) for o in (*others, *after)])


def swapped(values, kx, ky, kc):
    pairs = [(i, i ^ (kx * 8 + ky * 2 + kc)) for i in range(PEERS)]
    return lax.ppermute(values, "sub", pairs)


def sum_over_owners(keep, send, coarse, basis):
    both = (F32, BF)
    total, narrow = add_parts(keep, [swapped(send, 0, 0, 1)], both)
    first = merge(0, coarse, basis, narrow)
    others = [swapped(narrow, k, 0, 0) for k in (3, 1, 2)]
    total, narrow = add_parts(total, others, both, (first,))
    second = merge(1, coarse, basis, narrow)
    others = [swapped(narrow, 0, k, 0) for k in (3, 1, 2)]
    (narrow,) = add_parts(total, others, (BF,), (second,))
    return narrow, swapped(narrow, 0, 0, 1), first, second


PIECES = 2
PIECE = OB * BLK // PIECES


def start_kernel(ids_v, own, other, first, second, start, out, coeff, blocks, value, ids, sem, ids_sem):
    ids_copy = pltpu.make_async_copy(ids_v, ids, ids_sem)
    ids_copy.start()
    core = lax.axis_index("sub") % 2
    coeff[core] = own[...]
    coeff[1 - core] = other[...]
    copies = []
    for n in range(PIECES):
        merged = (first, second)[n]
        value[n] = jnp.dot(coeff[...].reshape(COLS, NB), merged[...], preferred_element_type=F32)
        copies.append(
            pltpu.make_async_copy(value.at[n], start.at[:, pl.ds(n * PIECE, PIECE)], sem.at[n])
        )
        copies[n].start()
        for k in range(PIECE // BLK):
            blocks[n * (PIECE // BLK) + k] = value[n, :, k * BLK : (k + 1) * BLK].astype(BF)
    ids_copy.wait()

    def peer(p, c):
        for q in range(CAP):
            g = jnp.maximum(ids[p, q], 0)
            out[p, q * COLS : (q + 1) * COLS, :] = blocks[g]
        return c

    lax.fori_loop(0, PEERS, peer, 0, unroll=2)
    for c in copies:
        c.wait()


def start_values(ids, own, other, first, second):
    return pl.pallas_call(
        start_kernel,
        out_shape=(
            jax.ShapeDtypeStruct((COLS, OB * BLK), F32),
            pltpu.VMEM((PEERS, SLOTROWS, BLK), BF),
        ),
        in_specs=[VMEM] * 5,
        out_specs=[HBM, VMEM],
        scratch_shapes=[
            pltpu.VMEM((2, HALF, NB), BF),
            pltpu.VMEM((OB, COLS, BLK), BF),
            pltpu.VMEM((PIECES, COLS, PIECE), F32),
            pltpu.SMEM((PEERS, BLK), jnp.int32),
            pltpu.SemaphoreType.DMA((PIECES,)),
            pltpu.SemaphoreType.DMA,
        ],
        compiler_params=params(8),
        name="start_values",
    )(in_vmem(ids), in_vmem(own), in_vmem(other), in_vmem(first), in_vmem(second))


def resid_kernel(ids_v, received, scale, dual, resid, t0, t1, t2, t3, value, ids, sem, ids_sem):
    ids_copy = pltpu.make_async_copy(ids_v, ids, ids_sem)
    ids_copy.start()
    totals = (t0, t1, t2, t3)
    zero_totals(totals)
    weight = 1.0 / (1.0 + scale[...].astype(F32))
    ids_copy.wait()
    add_slots(received, ids, totals)
    copies = []
    for n in range(PIECES):
        for k in range(PIECE // BLK):
            b = n * (PIECE // BLK) + k
            value[n, :, k * BLK : (k + 1) * BLK] = (
                dual[b] - sum_totals(totals, b) * weight[b : b + 1, :]
            )
        copies.append(
            pltpu.make_async_copy(value.at[n], resid.at[:, pl.ds(n * PIECE, PIECE)], sem.at[n])
        )
        copies[n].start()
    for c in copies:
        c.wait()


def residual(ids, received, scale, dual):
    return pl.pallas_call(
        resid_kernel,
        out_shape=jax.ShapeDtypeStruct((COLS, OB * BLK), F32),
        in_specs=[VMEM] * 4,
        out_specs=HBM,
        scratch_shapes=TOTALS
        + [
            pltpu.VMEM((PIECES, COLS, PIECE), F32),
            pltpu.SMEM((PEERS, BLK), jnp.int32),
            pltpu.SemaphoreType.DMA((PIECES,)),
            pltpu.SemaphoreType.DMA,
        ],
        compiler_params=params(8),
        name="residual",
    )(in_vmem(ids), in_vmem(received), scale, in_vmem(dual))


def exchange(values):
    return lax.all_to_all(values, "sub", split_axis=0, concat_axis=0, tiled=True)


def per_device(loads, operators, owner, dual_block, scale_index, basis, coarse):
    scale = scale_index.reshape(OB, BLK)
    packed, pos, ops_v = first_apply(owner.reshape(NBLK), dual_block, loads, operators)
    received = exchange(packed)
    dual, keep, send, ids, coarse_v = project(received, scale, basis, coarse)
    own, other, first, second = sum_over_owners(keep, send, coarse_v, basis)
    start, requested = start_values(ids, own, other, first, second)
    again = second_apply(pos, exchange(requested), ops_v)
    return (start, residual(ids, exchange(again), scale, dual))


def solution(mesh):
    return jax.shard_map(
        per_device,
        mesh=mesh,
        in_specs=(
            P("sub", "rep", None),
            P("sub", None, None),
            P("sub", None),
            P("sub"),
            P("sub"),
            P("sub", None),
            P(),
        ),
        out_specs=(P("rep", "sub"), P("rep", "sub")),
        check_vma=False,
    )
```

```python
import functools

import jax
import jax.numpy as jnp
from jax import lax
from jax.experimental import pallas as pl
from jax.experimental.pallas import tpu as pltpu
from jax.sharding import PartitionSpec as P

BLK = 128
PEERS = 32
CAP = 4
COLS = 64
HALF = COLS // 2
L = 1024
BPS = 8
NSUB = 8
NBLK = NSUB * BPS
OB = 16
MERGE = OB * BLK // 2
NB = 1024
IDROWS = 8
SLOTROWS = CAP * COLS
BF = jnp.bfloat16
F32 = jnp.float32
HBM = pl.BlockSpec(memory_space=pl.ANY)
SMEM = pl.BlockSpec(memory_space=pltpu.SMEM)
VMEM = pl.BlockSpec(memory_space=pltpu.VMEM)
AHEAD = 5


def params(mib):
    return pltpu.CompilerParams(vmem_limit_bytes=mib * 1024 * 1024)


def in_hbm(x):
    return pltpu.with_memory_space_constraint(x, pltpu.HBM)


def in_vmem(x):
    return pltpu.with_memory_space_constraint(x, pltpu.VMEM)


def slot(ref, p):
    return ref.at[p // CAP, pl.ds(pl.multiple_of((p % CAP) * COLS, COLS), COLS)]


def first_kernel(owner_h, block_h, loads, ops, out, pos, ops_v, owner, dual_block, count, loads_v, sem, load_sem, idx_sem):
    owner_copy = pltpu.make_async_copy(owner_h, owner, idx_sem.at[0])
    block_copy = pltpu.make_async_copy(block_h, dual_block, idx_sem.at[1])
    owner_copy.start()
    block_copy.start()
    load_copies = [
        pltpu.make_async_copy(loads.at[s], loads_v.at[s], load_sem.at[s]) for s in range(NSUB)
    ]
    copies = [pltpu.make_async_copy(ops.at[s], ops_v.at[s], sem.at[s]) for s in range(NSUB)]
    for s in range(AHEAD):
        load_copies[s].start()
        copies[s].start()

    def zero(i, c):
        count[i] = 0
        return c

    lax.fori_loop(0, PEERS, zero, 0)
    owner_copy.wait()
    block_copy.wait()
    row = lax.broadcasted_iota(jnp.int32, (PEERS, BLK), 0)
    lane = lax.broadcasted_iota(jnp.int32, (PEERS, BLK), 1)
    flat = jnp.where(lane < CAP, row * CAP + lane, -1)

    def rank(i, ids):
        d = owner[i]
        r = count[d]
        count[d] = r + 1
        p = d * CAP + r
        pos[i] = p
        return jnp.where(flat == p, dual_block[i], ids)

    ids = lax.fori_loop(0, NBLK, rank, jnp.full((PEERS, BLK), -1, jnp.int32))
    out[:, SLOTROWS : SLOTROWS + IDROWS, :] = jnp.broadcast_to(
        ids.astype(F32)[:, None, :], (PEERS, IDROWS, BLK)
    ).astype(BF)
    for s in range(NSUB):
        load_copies[s].wait()
        copies[s].wait()
        if s + AHEAD < NSUB:
            load_copies[s + AHEAD].start()
            copies[s + AHEAD].start()
        prod = jnp.dot(loads_v[s], ops_v[s], preferred_element_type=F32)
        for j in range(BPS):
            slot(out, pos[s * BPS + j])[...] = prod[:, j * BLK : (j + 1) * BLK].astype(BF)


def first_apply(owner, dual_block, loads, operators):
    return pl.pallas_call(
        first_kernel,
        out_shape=(
            pltpu.VMEM((PEERS, SLOTROWS + IDROWS, BLK), BF),
            jax.ShapeDtypeStruct((NBLK,), jnp.int32),
            pltpu.VMEM((NSUB, L, L), BF),
        ),
        in_specs=[HBM] * 4,
        out_specs=[VMEM, SMEM, VMEM],
        scratch_shapes=[
            pltpu.SMEM((NBLK,), jnp.int32),
            pltpu.SMEM((NBLK,), jnp.int32),
            pltpu.SMEM((PEERS,), jnp.int32),
            pltpu.VMEM((NSUB, COLS, L), BF),
            pltpu.SemaphoreType.DMA((NSUB,)),
            pltpu.SemaphoreType.DMA((NSUB,)),
            pltpu.SemaphoreType.DMA((2,)),
        ],
        compiler_params=params(8),
        name="first_apply",
    )(in_hbm(owner), in_hbm(dual_block), in_hbm(loads), in_hbm(operators))


def second_kernel(pos, back, ops, out):
    for s in range(NSUB):
        local = jnp.concatenate([slot(back, pos[s * BPS + j])[...] for j in range(BPS)], axis=1)
        prod = jnp.dot(local, ops[s], preferred_element_type=F32)
        for j in range(BPS):
            slot(out, pos[s * BPS + j])[...] = prod[:, j * BLK : (j + 1) * BLK].astype(BF)


def second_apply(pos, back, operators):
    return pl.pallas_call(
        second_kernel,
        out_shape=pltpu.VMEM((PEERS, SLOTROWS, BLK), BF),
        in_specs=[SMEM, VMEM, VMEM],
        out_specs=VMEM,
        compiler_params=params(8),
        name="second_apply",
    )(pos, in_vmem(back), in_vmem(operators))


def merge_kernel(part, coarse, basis, after, merged):
    for k in range(4):
        rows = slice(part * MERGE + k * 256, part * MERGE + (k + 1) * 256)
        merged[:, k * 256 : (k + 1) * 256] = lax.dot_general(
            coarse[...], basis[rows, :], (((1,), (1,)), ((), ())), preferred_element_type=F32
        ).astype(BF)


def merge(part, coarse, basis, after):
    return pl.pallas_call(
        functools.partial(merge_kernel, part),
        out_shape=pltpu.VMEM((NB, MERGE), BF),
        in_specs=[VMEM] * 3,
        out_specs=VMEM,
        compiler_params=params(6),
        name="merge",
    )(in_vmem(coarse), in_vmem(basis), in_vmem(after))


def zero_totals(totals):
    for q in range(CAP):
        totals[q][...] = jnp.zeros(totals[q].shape, F32)


def add_slots(received, ids, totals):
    def peer(p, c):
        for q in range(CAP):
            g = ids[p, q]
            g = jnp.where(g < 0, OB, g)
            totals[q][g] = totals[q][g] + received[p, q * COLS : (q + 1) * COLS, :].astype(F32)
        return c

    lax.fori_loop(0, PEERS, peer, 0, unroll=2)


def sum_totals(totals, b):
    return (totals[0][b] + totals[1][b]) + (totals[2][b] + totals[3][b])


TOTALS = [pltpu.VMEM((OB + 1, COLS, BLK), F32)] * CAP


def project_kernel(received, scale, basis, coarse, dual, keep, send, ids_out, coarse_v, t0, t1, t2, t3, narrow, idv, ids, sem, coarse_sem):
    coarse_copy = pltpu.make_async_copy(coarse, coarse_v, coarse_sem)
    coarse_copy.start()
    totals = (t0, t1, t2, t3)
    idv[...] = received[:, SLOTROWS : SLOTROWS + IDROWS, :].astype(F32)[:, 0, :].astype(jnp.int32)
    ids_copy = pltpu.make_async_copy(idv, ids, sem)
    ids_copy.start()
    ids_out[...] = idv[...]
    zero_totals(totals)
    ids_copy.wait()
    add_slots(received, ids, totals)
    weight = 1.0 / (1.0 + scale[...].astype(F32))
    for b in range(OB):
        owned = sum_totals(totals, b) * weight[b : b + 1, :]
        dual[b] = owned
        narrow[:, b * BLK : (b + 1) * BLK] = owned.astype(BF)
    product = jnp.dot(narrow[...], basis[...], preferred_element_type=F32)
    even = lax.axis_index("sub") % 2 == 0
    keep[...] = jnp.where(even, product[:HALF], product[HALF:])
    send[...] = jnp.where(even, product[HALF:], product[:HALF])
    coarse_copy.wait()


def project(received, scale, basis, coarse):
    return pl.pallas_call(
        project_kernel,
        out_shape=(
            pltpu.VMEM((OB, COLS, BLK), F32),
            pltpu.VMEM((HALF, NB), F32),
            pltpu.VMEM((HALF, NB), F32),
            pltpu.VMEM((PEERS, BLK), jnp.int32),
            pltpu.VMEM((NB, NB), BF),
        ),
        in_specs=[VMEM] * 3 + [HBM],
        out_specs=[VMEM] * 5,
        scratch_shapes=TOTALS
        + [
            pltpu.VMEM((COLS, OB * BLK), BF),
            pltpu.VMEM((PEERS, BLK), jnp.int32),
            pltpu.SMEM((PEERS, BLK), jnp.int32),
            pltpu.SemaphoreType.DMA,
            pltpu.SemaphoreType.DMA,
        ],
        compiler_params=params(8),
        name="project",
    )(in_vmem(received), scale, in_vmem(basis), in_hbm(coarse))


def add_kernel(count, inputs, *refs):
    total = refs[0][...]
    for other in refs[1:count]:
        total = total + other[...].astype(F32)
    for out in refs[inputs:]:
        out[...] = total.astype(out.dtype)


def add_parts(own, others, types, after=()):
    count = 1 + len(others)
    inputs = count + len(after)
    return pl.pallas_call(
        functools.partial(add_kernel, count, inputs),
        out_shape=[pltpu.VMEM((HALF, NB), t) for t in types],
        in_specs=[VMEM] * inputs,
        out_specs=[VMEM] * len(types),
        compiler_params=params(4),
        name="add_parts",
    )(in_vmem(own), *[in_vmem(o) for o in (*others, *after)])


def swapped(values, kx, ky, kc):
    pairs = [(i, i ^ (kx * 8 + ky * 2 + kc)) for i in range(PEERS)]
    return lax.ppermute(values, "sub", pairs)


def sum_over_owners(keep, send, coarse, basis):
    both = (F32, BF)
    total, narrow = add_parts(keep, [swapped(send, 0, 0, 1)], both)
    first = merge(0, coarse, basis, narrow)
    others = [swapped(narrow, k, 0, 0) for k in (3, 1, 2)]
    total, narrow = add_parts(total, others, both, (first,))
    second = merge(1, coarse, basis, narrow)
    others = [swapped(narrow, 0, k, 0) for k in (3, 1, 2)]
    (narrow,) = add_parts(total, others, (BF,), (second,))
    return narrow, swapped(narrow, 0, 0, 1), first, second


PIECES = 2
PIECE = OB * BLK // PIECES


def start_kernel(ids_v, own, other, first, second, start, out, blocks, value, ids, sem, ids_sem):
    ids_copy = pltpu.make_async_copy(ids_v, ids, ids_sem)
    ids_copy.start()
    even = lax.axis_index("sub") % 2 == 0
    coeff = jnp.concatenate(
        [jnp.where(even, own[...], other[...]), jnp.where(even, other[...], own[...])], axis=0
    )
    copies = []
    for n in range(PIECES):
        merged = (first, second)[n]
        value[n] = jnp.dot(coeff, merged[...], preferred_element_type=F32)
        copies.append(
            pltpu.make_async_copy(value.at[n], start.at[:, pl.ds(n * PIECE, PIECE)], sem.at[n])
        )
        copies[n].start()
        for k in range(PIECE // BLK):
            blocks[n * (PIECE // BLK) + k] = value[n, :, k * BLK : (k + 1) * BLK].astype(BF)
    ids_copy.wait()

    def peer(p, c):
        for q in range(CAP):
            g = jnp.maximum(ids[p, q], 0)
            out[p, q * COLS : (q + 1) * COLS, :] = blocks[g]
        return c

    lax.fori_loop(0, PEERS, peer, 0, unroll=2)
    for c in copies:
        c.wait()


def start_values(ids, own, other, first, second):
    return pl.pallas_call(
        start_kernel,
        out_shape=(
            jax.ShapeDtypeStruct((COLS, OB * BLK), F32),
            pltpu.VMEM((PEERS, SLOTROWS, BLK), BF),
        ),
        in_specs=[VMEM] * 5,
        out_specs=[HBM, VMEM],
        scratch_shapes=[
            pltpu.VMEM((OB, COLS, BLK), BF),
            pltpu.VMEM((PIECES, COLS, PIECE), F32),
            pltpu.SMEM((PEERS, BLK), jnp.int32),
            pltpu.SemaphoreType.DMA((PIECES,)),
            pltpu.SemaphoreType.DMA,
        ],
        compiler_params=params(8),
        name="start_values",
    )(in_vmem(ids), in_vmem(own), in_vmem(other), in_vmem(first), in_vmem(second))


def resid_kernel(ids_v, received, scale, dual, resid, t0, t1, t2, t3, value, ids, sem, ids_sem):
    ids_copy = pltpu.make_async_copy(ids_v, ids, ids_sem)
    ids_copy.start()
    totals = (t0, t1, t2, t3)
    zero_totals(totals)
    weight = 1.0 / (1.0 + scale[...].astype(F32))
    ids_copy.wait()
    add_slots(received, ids, totals)
    copies = []
    for n in range(PIECES):
        for k in range(PIECE // BLK):
            b = n * (PIECE // BLK) + k
            value[n, :, k * BLK : (k + 1) * BLK] = (
                dual[b] - sum_totals(totals, b) * weight[b : b + 1, :]
            )
        copies.append(
            pltpu.make_async_copy(value.at[n], resid.at[:, pl.ds(n * PIECE, PIECE)], sem.at[n])
        )
        copies[n].start()
    for c in copies:
        c.wait()


def residual(ids, received, scale, dual):
    return pl.pallas_call(
        resid_kernel,
        out_shape=jax.ShapeDtypeStruct((COLS, OB * BLK), F32),
        in_specs=[VMEM] * 4,
        out_specs=HBM,
        scratch_shapes=TOTALS
        + [
            pltpu.VMEM((PIECES, COLS, PIECE), F32),
            pltpu.SMEM((PEERS, BLK), jnp.int32),
            pltpu.SemaphoreType.DMA((PIECES,)),
            pltpu.SemaphoreType.DMA,
        ],
        compiler_params=params(8),
        name="residual",
    )(in_vmem(ids), in_vmem(received), scale, in_vmem(dual))


def exchange(values):
    return lax.all_to_all(values, "sub", split_axis=0, concat_axis=0, tiled=True)


def per_device(loads, operators, owner, dual_block, scale_index, basis, coarse):
    scale = scale_index.reshape(OB, BLK)
    packed, pos, ops_v = first_apply(owner.reshape(NBLK), dual_block, loads, operators)
    received = exchange(packed)
    dual, keep, send, ids, coarse_v = project(received, scale, basis, coarse)
    own, other, first, second = sum_over_owners(keep, send, coarse_v, basis)
    start, requested = start_values(ids, own, other, first, second)
    again = second_apply(pos, exchange(requested), ops_v)
    return (start, residual(ids, exchange(again), scale, dual))


def solution(mesh):
    return jax.shard_map(
        per_device,
        mesh=mesh,
        in_specs=(
            P("sub", "rep", None),
            P("sub", None, None),
            P("sub", None),
            P("sub"),
            P("sub"),
            P("sub", None),
            P(),
        ),
        out_specs=(P("rep", "sub"), P("rep", "sub")),
        check_vma=False,
    )
```

```python
import functools

import jax
import jax.numpy as jnp
from jax import lax
from jax.experimental import pallas as pl
from jax.experimental.pallas import tpu as pltpu
from jax.sharding import PartitionSpec as P

BLK = 128
PEERS = 32
CAP = 4
COLS = 64
HALF = COLS // 2
L = 1024
BPS = 8
NSUB = 8
NBLK = NSUB * BPS
OB = 16
MERGE = OB * BLK // 2
NB = 1024
IDROWS = 8
SLOTROWS = CAP * COLS
BF = jnp.bfloat16
F32 = jnp.float32
HBM = pl.BlockSpec(memory_space=pl.ANY)
SMEM = pl.BlockSpec(memory_space=pltpu.SMEM)
VMEM = pl.BlockSpec(memory_space=pltpu.VMEM)
AHEAD = 5


def params(mib):
    return pltpu.CompilerParams(vmem_limit_bytes=mib * 1024 * 1024)


def in_hbm(x):
    return pltpu.with_memory_space_constraint(x, pltpu.HBM)


def in_vmem(x):
    return pltpu.with_memory_space_constraint(x, pltpu.VMEM)


def slot(ref, p):
    return ref.at[p // CAP, pl.ds(pl.multiple_of((p % CAP) * COLS, COLS), COLS)]


def first_kernel(owner_h, block_h, loads, ops, out, pos, ops_v, owner, dual_block, count, loads_v, sem, load_sem, idx_sem):
    owner_copy = pltpu.make_async_copy(owner_h, owner, idx_sem.at[0])
    block_copy = pltpu.make_async_copy(block_h, dual_block, idx_sem.at[1])
    owner_copy.start()
    block_copy.start()
    load_copies = [
        pltpu.make_async_copy(loads.at[s], loads_v.at[s], load_sem.at[s]) for s in range(NSUB)
    ]
    copies = [pltpu.make_async_copy(ops.at[s], ops_v.at[s], sem.at[s]) for s in range(NSUB)]
    for s in range(AHEAD):
        load_copies[s].start()
        copies[s].start()

    def zero(i, c):
        count[i] = 0
        return c

    lax.fori_loop(0, PEERS, zero, 0)
    owner_copy.wait()
    block_copy.wait()
    row = lax.broadcasted_iota(jnp.int32, (PEERS, BLK), 0)
    lane = lax.broadcasted_iota(jnp.int32, (PEERS, BLK), 1)
    flat = jnp.where(lane < CAP, row * CAP + lane, -1)

    def rank(i, ids):
        d = owner[i]
        r = count[d]
        count[d] = r + 1
        p = d * CAP + r
        pos[i] = p
        return jnp.where(flat == p, dual_block[i], ids)

    ids = lax.fori_loop(0, NBLK, rank, jnp.full((PEERS, BLK), -1, jnp.int32))
    out[:, SLOTROWS : SLOTROWS + IDROWS, :] = jnp.broadcast_to(
        ids.astype(F32)[:, None, :], (PEERS, IDROWS, BLK)
    ).astype(BF)
    for s in range(NSUB):
        load_copies[s].wait()
        copies[s].wait()
        if s + AHEAD < NSUB:
            load_copies[s + AHEAD].start()
            copies[s + AHEAD].start()
        prod = jnp.dot(loads_v[s], ops_v[s], preferred_element_type=F32)
        for j in range(BPS):
            slot(out, pos[s * BPS + j])[...] = prod[:, j * BLK : (j + 1) * BLK].astype(BF)


def first_apply(owner, dual_block, loads, operators):
    return pl.pallas_call(
        first_kernel,
        out_shape=(
            pltpu.VMEM((PEERS, SLOTROWS + IDROWS, BLK), BF),
            jax.ShapeDtypeStruct((NBLK,), jnp.int32),
            pltpu.VMEM((NSUB, L, L), BF),
        ),
        in_specs=[HBM] * 4,
        out_specs=[VMEM, SMEM, VMEM],
        scratch_shapes=[
            pltpu.SMEM((NBLK,), jnp.int32),
            pltpu.SMEM((NBLK,), jnp.int32),
            pltpu.SMEM((PEERS,), jnp.int32),
            pltpu.VMEM((NSUB, COLS, L), BF),
            pltpu.SemaphoreType.DMA((NSUB,)),
            pltpu.SemaphoreType.DMA((NSUB,)),
            pltpu.SemaphoreType.DMA((2,)),
        ],
        compiler_params=params(8),
        name="first_apply",
    )(in_hbm(owner), in_hbm(dual_block), in_hbm(loads), in_hbm(operators))


def second_kernel(pos, back, ops, out):
    for s in range(NSUB):
        local = jnp.concatenate([slot(back, pos[s * BPS + j])[...] for j in range(BPS)], axis=1)
        prod = jnp.dot(local, ops[s], preferred_element_type=F32)
        for j in range(BPS):
            slot(out, pos[s * BPS + j])[...] = prod[:, j * BLK : (j + 1) * BLK].astype(BF)


def second_apply(pos, back, operators):
    return pl.pallas_call(
        second_kernel,
        out_shape=pltpu.VMEM((PEERS, SLOTROWS, BLK), BF),
        in_specs=[SMEM, VMEM, VMEM],
        out_specs=VMEM,
        compiler_params=params(8),
        name="second_apply",
    )(pos, in_vmem(back), in_vmem(operators))


def merge_kernel(part, coarse, basis, after, merged):
    for k in range(4):
        rows = slice(part * MERGE + k * 256, part * MERGE + (k + 1) * 256)
        merged[:, k * 256 : (k + 1) * 256] = lax.dot_general(
            coarse[...], basis[rows, :], (((1,), (1,)), ((), ())), preferred_element_type=F32
        ).astype(BF)


def merge(part, coarse, basis, after):
    return pl.pallas_call(
        functools.partial(merge_kernel, part),
        out_shape=pltpu.VMEM((NB, MERGE), BF),
        in_specs=[VMEM] * 3,
        out_specs=VMEM,
        compiler_params=params(6),
        name="merge",
    )(in_vmem(coarse), in_vmem(basis), in_vmem(after))


def zero_totals(totals):
    for q in range(CAP):
        totals[q][...] = jnp.zeros(totals[q].shape, F32)


def add_slots(received, ids, totals):
    def peer(p, c):
        for q in range(CAP):
            g = ids[p, q]
            g = jnp.where(g < 0, OB, g)
            totals[q][g] = totals[q][g] + received[p, q * COLS : (q + 1) * COLS, :].astype(F32)
        return c

    lax.fori_loop(0, PEERS, peer, 0, unroll=4)


def sum_totals(totals, b):
    return (totals[0][b] + totals[1][b]) + (totals[2][b] + totals[3][b])


TOTALS = [pltpu.VMEM((OB + 1, COLS, BLK), F32)] * CAP


def project_kernel(received, scale, basis, coarse, dual, keep, send, ids_out, coarse_v, t0, t1, t2, t3, narrow, idv, ids, sem, coarse_sem):
    coarse_copy = pltpu.make_async_copy(coarse, coarse_v, coarse_sem)
    coarse_copy.start()
    totals = (t0, t1, t2, t3)
    idv[...] = received[:, SLOTROWS : SLOTROWS + IDROWS, :].astype(F32)[:, 0, :].astype(jnp.int32)
    ids_copy = pltpu.make_async_copy(idv, ids, sem)
    ids_copy.start()
    ids_out[...] = idv[...]
    zero_totals(totals)
    ids_copy.wait()
    add_slots(received, ids, totals)
    weight = 1.0 / (1.0 + scale[...].astype(F32))
    for b in range(OB):
        owned = sum_totals(totals, b) * weight[b : b + 1, :]
        dual[b] = owned
        narrow[:, b * BLK : (b + 1) * BLK] = owned.astype(BF)
    product = jnp.dot(narrow[...], basis[...], preferred_element_type=F32)
    even = lax.axis_index("sub") % 2 == 0
    keep[...] = jnp.where(even, product[:HALF], product[HALF:])
    send[...] = jnp.where(even, product[HALF:], product[:HALF])
    coarse_copy.wait()


def project(received, scale, basis, coarse):
    return pl.pallas_call(
        project_kernel,
        out_shape=(
            pltpu.VMEM((OB, COLS, BLK), F32),
            pltpu.VMEM((HALF, NB), F32),
            pltpu.VMEM((HALF, NB), F32),
            pltpu.VMEM((PEERS, BLK), jnp.int32),
            pltpu.VMEM((NB, NB), BF),
        ),
        in_specs=[VMEM] * 3 + [HBM],
        out_specs=[VMEM] * 5,
        scratch_shapes=TOTALS
        + [
            pltpu.VMEM((COLS, OB * BLK), BF),
            pltpu.VMEM((PEERS, BLK), jnp.int32),
            pltpu.SMEM((PEERS, BLK), jnp.int32),
            pltpu.SemaphoreType.DMA,
            pltpu.SemaphoreType.DMA,
        ],
        compiler_params=params(8),
        name="project",
    )(in_vmem(received), scale, in_vmem(basis), in_hbm(coarse))


def add_kernel(count, inputs, *refs):
    total = refs[0][...]
    for other in refs[1:count]:
        total = total + other[...].astype(F32)
    for out in refs[inputs:]:
        out[...] = total.astype(out.dtype)


def add_parts(own, others, types, after=()):
    count = 1 + len(others)
    inputs = count + len(after)
    return pl.pallas_call(
        functools.partial(add_kernel, count, inputs),
        out_shape=[pltpu.VMEM((HALF, NB), t) for t in types],
        in_specs=[VMEM] * inputs,
        out_specs=[VMEM] * len(types),
        compiler_params=params(4),
        name="add_parts",
    )(in_vmem(own), *[in_vmem(o) for o in (*others, *after)])


def swapped(values, kx, ky, kc):
    pairs = [(i, i ^ (kx * 8 + ky * 2 + kc)) for i in range(PEERS)]
    return lax.ppermute(values, "sub", pairs)


def sum_over_owners(keep, send, coarse, basis):
    both = (F32, BF)
    total, narrow = add_parts(keep, [swapped(send, 0, 0, 1)], both)
    first = merge(0, coarse, basis, narrow)
    others = [swapped(narrow, k, 0, 0) for k in (3, 1, 2)]
    total, narrow = add_parts(total, others, both, (first,))
    second = merge(1, coarse, basis, narrow)
    others = [swapped(narrow, 0, k, 0) for k in (3, 1, 2)]
    (narrow,) = add_parts(total, others, (BF,), (second,))
    return narrow, swapped(narrow, 0, 0, 1), first, second


PIECES = 2
PIECE = OB * BLK // PIECES


def start_kernel(ids_v, own, other, first, second, start, out, blocks, value, ids, sem, ids_sem):
    ids_copy = pltpu.make_async_copy(ids_v, ids, ids_sem)
    ids_copy.start()
    even = lax.axis_index("sub") % 2 == 0
    coeff = jnp.concatenate(
        [jnp.where(even, own[...], other[...]), jnp.where(even, other[...], own[...])], axis=0
    )
    copies = []
    for n in range(PIECES):
        merged = (first, second)[n]
        value[n] = jnp.dot(coeff, merged[...], preferred_element_type=F32)
        copies.append(
            pltpu.make_async_copy(value.at[n], start.at[:, pl.ds(n * PIECE, PIECE)], sem.at[n])
        )
        copies[n].start()
        for k in range(PIECE // BLK):
            blocks[n * (PIECE // BLK) + k] = value[n, :, k * BLK : (k + 1) * BLK].astype(BF)
    ids_copy.wait()

    def peer(p, c):
        for q in range(CAP):
            g = jnp.maximum(ids[p, q], 0)
            out[p, q * COLS : (q + 1) * COLS, :] = blocks[g]
        return c

    lax.fori_loop(0, PEERS, peer, 0, unroll=4)
    for c in copies:
        c.wait()


def start_values(ids, own, other, first, second):
    return pl.pallas_call(
        start_kernel,
        out_shape=(
            jax.ShapeDtypeStruct((COLS, OB * BLK), F32),
            pltpu.VMEM((PEERS, SLOTROWS, BLK), BF),
        ),
        in_specs=[VMEM] * 5,
        out_specs=[HBM, VMEM],
        scratch_shapes=[
            pltpu.VMEM((OB, COLS, BLK), BF),
            pltpu.VMEM((PIECES, COLS, PIECE), F32),
            pltpu.SMEM((PEERS, BLK), jnp.int32),
            pltpu.SemaphoreType.DMA((PIECES,)),
            pltpu.SemaphoreType.DMA,
        ],
        compiler_params=params(8),
        name="start_values",
    )(in_vmem(ids), in_vmem(own), in_vmem(other), in_vmem(first), in_vmem(second))


def resid_kernel(ids_v, received, scale, dual, resid, t0, t1, t2, t3, value, ids, sem, ids_sem):
    ids_copy = pltpu.make_async_copy(ids_v, ids, ids_sem)
    ids_copy.start()
    totals = (t0, t1, t2, t3)
    zero_totals(totals)
    weight = 1.0 / (1.0 + scale[...].astype(F32))
    ids_copy.wait()
    add_slots(received, ids, totals)
    copies = []
    for n in range(PIECES):
        for k in range(PIECE // BLK):
            b = n * (PIECE // BLK) + k
            value[n, :, k * BLK : (k + 1) * BLK] = (
                dual[b] - sum_totals(totals, b) * weight[b : b + 1, :]
            )
        copies.append(
            pltpu.make_async_copy(value.at[n], resid.at[:, pl.ds(n * PIECE, PIECE)], sem.at[n])
        )
        copies[n].start()
    for c in copies:
        c.wait()


def residual(ids, received, scale, dual):
    return pl.pallas_call(
        resid_kernel,
        out_shape=jax.ShapeDtypeStruct((COLS, OB * BLK), F32),
        in_specs=[VMEM] * 4,
        out_specs=HBM,
        scratch_shapes=TOTALS
        + [
            pltpu.VMEM((PIECES, COLS, PIECE), F32),
            pltpu.SMEM((PEERS, BLK), jnp.int32),
            pltpu.SemaphoreType.DMA((PIECES,)),
            pltpu.SemaphoreType.DMA,
        ],
        compiler_params=params(8),
        name="residual",
    )(in_vmem(ids), in_vmem(received), scale, in_vmem(dual))


def exchange(values):
    return lax.all_to_all(values, "sub", split_axis=0, concat_axis=0, tiled=True)


def per_device(loads, operators, owner, dual_block, scale_index, basis, coarse):
    scale = scale_index.reshape(OB, BLK)
    packed, pos, ops_v = first_apply(owner.reshape(NBLK), dual_block, loads, operators)
    received = exchange(packed)
    dual, keep, send, ids, coarse_v = project(received, scale, basis, coarse)
    own, other, first, second = sum_over_owners(keep, send, coarse_v, basis)
    start, requested = start_values(ids, own, other, first, second)
    again = second_apply(pos, exchange(requested), ops_v)
    return (start, residual(ids, exchange(again), scale, dual))


def solution(mesh):
    return jax.shard_map(
        per_device,
        mesh=mesh,
        in_specs=(
            P("sub", "rep", None),
            P("sub", None, None),
            P("sub", None),
            P("sub"),
            P("sub"),
            P("sub", None),
            P(),
        ),
        out_specs=(P("rep", "sub"), P("rep", "sub")),
        check_vma=False,
    )
```
